1024 devices in a mesh: dom: 64 (over y, z_lo), orb: 16 (over x, z_hi, core).
Axes of the slice: x: 4, y: 8, z: 16 (z_hi: 2, z_lo: 8; z = z_hi * 8 + z_lo), core: 2. Of those that a mesh axis runs over, the one named last changes fastest.
Arguments:
- orbitals: bfloat16 [150528, 1024], P('dom', 'orb'), may hold values from -16 to 16
- potential: float32 [150528], P('dom'), may hold values from 0.5 to 2
- cell_hamiltonian: bfloat16 [512, 343, 343], P('dom'), may hold values from -2 to 2, as said below
- connectivity: int32 [512, 343], P('dom'), may hold values from 0 to 2400, as said below
- face_nodes: int32 [3136], P('dom'), may hold values from 0 to 2351, as said below
Outputs:
- residual: float32 [150528, 1024], P(('dom', 'orb'))
- projected: bfloat16 [1024, 1024], replicated
The draws below stay inside these ranges and needn't reach their ends.
Inputs may be any that keep to these rules, and one draw needn't show every extreme that they name: `connectivity`: cell c of a domain is its c-th layer of cells; each row lists the cell's 343 nodes in the domain's local numbering, where a number 2352 + p stands for entry p of the next domain's face_nodes list. Every local node of a domain belongs to some cell of it, and neighbouring cells of a domain share a face of 49 nodes. `face_nodes`: each domain's 49 entries are distinct local node numbers of that domain: the nodes that the previous domain's last cell shares with it, in the order of that cell's numbers 2352 + p. `cell_hamiltonian`: each cell's matrix is symmetric.
All inputs are finite; a program needn't handle non-finite values.
Results may differ from the reference program's by a relative error of at most 0.0096.
Values may be sent and summed in bfloat16 or wider, within the bound.
A program may use at most 32 MiB of HBM per device.

```python
import math
import jax
import jax.numpy as jnp
from jax import lax

ORDER = 6
NPC = 343
FACE = 49
KZ = 8
NODE_DEV = 2352
ORBITALS = 1024
DEGREE = 4
CELLS = 512
NODES = 150528


def swap_values(perm, first, second):
    return jnp.where(perm == first, second, jnp.where(perm == second, first, perm)).astype(jnp.int32)


def domain_perm(sub):
    raw = jax.random.permutation(sub, NODE_DEV).astype(jnp.int32)
    raw = swap_values(raw, raw[0], NODE_DEV - 1)
    raw = swap_values(raw, raw[1], 0)
    return raw


def mesh_tables(key):
    domains = CELLS // KZ
    keys = jax.random.split(jax.random.fold_in(key, 7), domains)
    perms = jax.vmap(domain_perm)(keys).astype(jnp.int32)
    cell = jnp.arange(KZ, dtype=jnp.int32)
    local = jnp.arange(NPC, dtype=jnp.int32)
    layer = ORDER * cell[:, None] + (local // FACE)[None, :]
    position = (local % FACE)[None, :] + 0 * layer
    natural = jnp.minimum(layer * FACE + position, NODE_DEV - 1)
    owned = jnp.take(perms, natural.reshape(-1), axis=1).reshape(domains, KZ, NPC)
    ghost = jnp.broadcast_to(NODE_DEV + position, (domains, KZ, NPC))
    top = jnp.broadcast_to(layer >= ORDER * KZ, (domains, KZ, NPC))
    conn = jnp.where(top, ghost, owned).astype(jnp.int32)
    faces = perms[:, :FACE]
    return (conn.reshape(CELLS, NPC), faces.reshape(-1).astype(jnp.int32))


def draw_connectivity(key, part):
    return mesh_tables(key)[0]


def draw_face_nodes(key, part):
    return mesh_tables(key)[1]


def draw_cell_hamiltonian(key, part):
    raw = jax.random.normal(jax.random.fold_in(key, 11), (CELLS, NPC, NPC), jnp.float32)
    sym = (raw + jnp.swapaxes(raw, 1, 2)) * (0.02 / 1.4142135)
    sym = jnp.clip(sym, -0.15, 0.15) + 0.3 * jnp.eye(NPC, dtype=jnp.float32)[None, :, :]
    return sym.astype(jnp.bfloat16)


def strengthened(values, stream_key, source, target, blocks, factor):
    def block_of(dim):
        return (jnp.arange(values.shape[dim]) // (values.shape[dim] // blocks)).reshape((-1,) + (1,) * (values.ndim - 1 - dim))

    near = jax.random.permutation(stream_key, blocks)[block_of(target)]
    other_side = (block_of(target) + blocks // 2) % blocks
    return jnp.where((block_of(source) == near) | (block_of(source) == other_side), factor * values, values)


def steps_of(stream_key, dims, shards, smallest, largest):
    loudness = 1.0
    for axis_at, parts in shards:
        heights = jax.random.uniform(jax.random.fold_in(jax.random.fold_in(stream_key, 6), axis_at), (parts,), jnp.float32, smallest / len(shards), largest / len(shards))
        loudness = loudness * jnp.repeat(jnp.exp(heights), dims[axis_at] // parts).reshape((-1,) + (1,) * (len(dims) - 1 - axis_at))
    return loudness


def gaussian_with(key, shape, deviation, limit, cuts, heavy, kind=jnp.bfloat16):
    entries = deviation * jax.random.normal(key, shape, jnp.float32)
    if cuts:
        entries = entries * steps_of(key, shape, cuts, -0.22, 0.18)
    return jnp.clip(strengthened(entries, jax.random.fold_in(key, 3), *heavy), -limit, limit).astype(kind)


def setup_inputs(seed: int = 0) -> dict:
    key_list = jax.random.split(jax.random.key(seed), 6)
    return {
        "orbitals": gaussian_with(key_list[0], (NODES, ORBITALS), 1.0, 16.0, ((0, 64), (1, 16)), (0, 1, 64, 4.0)),
        "potential": jnp.clip(jnp.exp(math.log(2.0) - 1.3862944 * jax.random.uniform(key_list[1], (NODES,), jnp.float32) ** steps_of(key_list[1], (NODES,), ((0, 64),), -0.2, 0.2)), 0.5, 2.0),
        "cell_hamiltonian": draw_cell_hamiltonian(jax.random.fold_in(key_list[5], 71), 0),
        "connectivity": draw_connectivity(jax.random.fold_in(key_list[5], 71), 0),
        "face_nodes": draw_face_nodes(jax.random.fold_in(key_list[5], 71), 0),
    }


filter_center = 1.5
filter_half = 2.0


def reference(orbitals, potential, cell_hamiltonian, connectivity, face_nodes):
    domains = CELLS // KZ
    owner = (jnp.arange(CELLS, dtype=jnp.int32) // KZ)[:, None]
    faces = face_nodes.reshape(domains, FACE)
    following = jnp.minimum(owner + 1, domains - 1)
    ghost_slot = jnp.clip(connectivity - NODE_DEV, 0, FACE - 1)
    ghost_node = faces[following, ghost_slot]
    remote = jnp.where(owner + 1 < domains, (owner + 1) * NODE_DEV + ghost_node, NODES)
    global_index = jnp.where(connectivity >= NODE_DEV, remote, owner * NODE_DEV + connectivity).astype(jnp.int32)
    cell_index = global_index.reshape(domains, KZ, NPC)
    matrices = cell_hamiltonian.reshape(domains, KZ, NPC, NPC)

    def apply_hamiltonian(values):
        padded = jnp.concatenate([values, jnp.zeros((1, ORBITALS), values.dtype)], axis=0)

        def add_domain(running, item):
            index, mats = item
            gathered = padded[index].astype(jnp.float32)
            products = jnp.einsum("kij,kjo->kio", mats.astype(jnp.float32), gathered)
            return running.at[index].add(products), None

        running, unused = lax.scan(add_domain, jnp.zeros((NODES + 1, ORBITALS), jnp.float32), (cell_index, matrices))
        return running[:NODES] + potential[:, None] * values.astype(jnp.float32)

    previous = orbitals
    image = apply_hamiltonian(previous)
    current = ((image - filter_center * previous.astype(jnp.float32)) / filter_half).astype(jnp.bfloat16)
    for step in range(DEGREE - 1):
        image = apply_hamiltonian(current)
        following_iter = (2.0 * (image - filter_center * current.astype(jnp.float32)) / filter_half - previous.astype(jnp.float32)).astype(jnp.bfloat16)
        previous, current = current, following_iter
    image = apply_hamiltonian(current).astype(jnp.bfloat16)
    projected = (jnp.dot(current.T, image, preferred_element_type=jnp.float32) / NODES).astype(jnp.bfloat16)
    residual = image.astype(jnp.float32) - jnp.dot(current, projected, preferred_element_type=jnp.float32)
    return residual, projected
```

```python
import functools

import jax
import jax.numpy as jnp
from jax import lax
from jax.experimental import pallas as pl
from jax.experimental.pallas import tpu as pltpu
from jax.sharding import PartitionSpec as P

DEGREE = 4
MESH = pl.DeviceIdType.MESH
F32 = jnp.float32
BF16 = jnp.bfloat16

filter_center = 1.5
filter_half = 2.0

SIDE = 64
STRIDE = 320
SPAN = STRIDE + SIDE


def prefix_tables(n):
    before = lax.broadcasted_iota(jnp.int32, (n, n), 0) < lax.broadcasted_iota(jnp.int32, (n, n), 1)
    after = lax.broadcasted_iota(jnp.int32, (n, n), 0) > lax.broadcasted_iota(jnp.int32, (n, n), 1)
    return before.astype(F32).astype(BF16), after.astype(F32).astype(BF16)


def dot(a, b):
    return jnp.dot(a, b, preferred_element_type=F32)


def equal(a, b):
    return (a == b).astype(F32)


def filter_kernel(
    sizes,
    nodes_ref,
    mats_ref,
    conn_ref,
    conn_col_ref,
    face_ref,
    face_col_ref,
    out_ref,
    values,
    cellmats,
    total,
    pots,
    ids_col,
    ids_row,
    both,
    ghosts,
    behind,
    behind_mat,
    send_sem,
    recv_sem,
    mat_sem,
):
    cells, npc, owned, share, blocks = sizes
    dom = lax.axis_index("dom")
    domains = lax.axis_size("dom")
    nxt = lax.rem(dom + 1, domains)
    prv = lax.rem(dom + domains - 1, domains)
    barrier = pltpu.get_barrier_semaphore()
    for other in (prv, nxt):
        pl.semaphore_signal(barrier, inc=1, device_id={"dom": other}, device_id_type=MESH)

    rows = [conn_ref[c : c + 1, :] for c in range(cells)]
    cols = [conn_col_ref[:, c : c + 1] for c in range(cells)]
    face_row, face_col = face_ref[...], face_col_ref[...]
    faces = face_row.shape[1]

    low = [equal(cols[c], rows[c + 1]) for c in range(cells - 1)]
    high = [equal(cols[c + 1], rows[c]) for c in range(cells - 1)]
    first_row = equal(face_col, rows[0])
    first_col = equal(cols[0], face_row)
    bottom_row = [jnp.sum(first_row, axis=0, keepdims=True)]
    bottom_row += [jnp.sum(low[c], axis=0, keepdims=True) for c in range(cells - 1)]
    bottom_col = [jnp.sum(first_col, axis=1, keepdims=True)]
    bottom_col += [jnp.sum(high[c], axis=1, keepdims=True) for c in range(cells - 1)]
    top_row = [jnp.sum(high[c], axis=0, keepdims=True) for c in range(cells - 1)]
    top_row += [(rows[-1] >= owned).astype(F32)]
    top_col = [jnp.sum(low[c], axis=1, keepdims=True) for c in range(cells - 1)]
    top_col += [(cols[-1] >= owned).astype(F32)]

    before, after = prefix_tables(npc)
    inner_row = [1.0 - bottom_row[c] - top_row[c] for c in range(cells)]
    inner_col = [1.0 - bottom_col[c] - top_col[c] for c in range(cells)]
    stacked_row = jnp.concatenate(bottom_row + inner_row, axis=0).astype(BF16)
    stacked_col = jnp.concatenate(bottom_col + inner_col, axis=1).astype(BF16)
    rank_row = dot(stacked_row, before)
    rank_col = dot(after, stacked_col)
    place_row = lax.broadcasted_iota(jnp.int32, (faces, 1), 0).astype(F32)
    place_col = lax.broadcasted_iota(jnp.int32, (1, faces), 1).astype(F32)
    low_row = [jnp.sum(first_row * place_row, axis=0, keepdims=True)]
    low_row += [rank_row[c : c + 1] for c in range(1, cells)]
    low_col = [jnp.sum(first_col * place_col, axis=1, keepdims=True)]
    low_col += [rank_col[:, c : c + 1] for c in range(1, cells)]
    high_row = [jnp.sum(high[c] * low_col[c + 1], axis=0, keepdims=True) for c in range(cells - 1)]
    high_row += [(rows[-1] - owned).astype(F32)]
    high_col = [jnp.sum(low[c] * low_row[c + 1], axis=1, keepdims=True) for c in range(cells - 1)]
    high_col += [(cols[-1] - owned).astype(F32)]

    def slots(bottom, top, low_rank, high_rank, inner_rank):
        inner = SIDE + inner_rank
        return jnp.where(bottom > 0.5, low_rank, jnp.where(top > 0.5, STRIDE + high_rank, inner)).astype(
            jnp.int32
        )

    def spread_of(c):
        slot_row = slots(
            bottom_row[c], top_row[c], low_row[c], high_row[c], rank_row[cells + c : cells + c + 1]
        )
        slot_col = slots(
            bottom_col[c], top_col[c], low_col[c], high_col[c], rank_col[:, cells + c : cells + c + 1]
        )
        down = equal(lax.broadcasted_iota(jnp.int32, (SPAN, npc), 0), slot_row)
        across = equal(slot_col, lax.broadcasted_iota(jnp.int32, (npc, SPAN), 1))
        return down, across

    order = [cells - 1] + list(range(cells - 1))
    for c in order:
        down, across = spread_of(c)
        named = rows[c].astype(F32) + 1.0
        ids_col[c] = (jnp.sum(down * named, axis=1, keepdims=True) - 1.0).astype(jnp.int32)
        named = cols[c].astype(F32) + 1.0
        ids_row[c] = (jnp.sum(across * named, axis=0, keepdims=True) - 1.0).astype(jnp.int32)
        half = dot(down.astype(BF16), mats_ref[c]).astype(BF16)
        cellmats[c] = dot(half, across.astype(BF16)).astype(BF16)

    pl.semaphore_wait(barrier, 2)
    mat_copy = pltpu.make_async_remote_copy(
        src_ref=cellmats.at[cells - 1, pl.ds(STRIDE, SIDE)],
        dst_ref=behind_mat,
        send_sem=mat_sem.at[0],
        recv_sem=mat_sem.at[1],
        device_id={"dom": nxt},
        device_id_type=MESH,
    )
    mat_copy.start()

    width = values.shape[2]

    def take(c, carry):
        pick = equal(
            ids_col[c, pl.ds(0, STRIDE), :], lax.broadcasted_iota(jnp.int32, (STRIDE, owned), 1)
        )
        found = dot(pick.astype(BF16), nodes_ref[...])
        start = pl.multiple_of(c * STRIDE, STRIDE)
        values[0, pl.ds(start, STRIDE), :] = found[:, :width].astype(BF16)
        pot = found[:, width : width + 1] + found[:, width + 1 : width + 2] + found[:, width + 2 : width + 3]
        pots[pl.ds(start, STRIDE), :] = jnp.broadcast_to(pot, (STRIDE, width))
        return carry

    lax.fori_loop(0, cells, take, 0)

    end = cells * STRIDE
    has_next = (dom < domains - 1).astype(F32)
    has_prev = (dom > 0).astype(F32)
    copies = []
    for step in range(DEGREE + 1):
        back = pltpu.make_async_remote_copy(
            src_ref=values.at[step, pl.ds(0, SIDE)],
            dst_ref=ghosts.at[step],
            send_sem=send_sem.at[step, 0],
            recv_sem=recv_sem.at[step, 0],
            device_id={"dom": prv},
            device_id_type=MESH,
        )
        ahead = pltpu.make_async_remote_copy(
            src_ref=values.at[step, pl.ds(end - STRIDE, STRIDE)],
            dst_ref=behind.at[step],
            send_sem=send_sem.at[step, 1],
            recv_sem=recv_sem.at[step, 1],
            device_id={"dom": nxt},
            device_id_type=MESH,
        )
        back.start()
        ahead.start()
        copies += [back, ahead]
        total[...] = jnp.zeros_like(total)
        for c in range(cells - 1):
            span = pl.ds(c * STRIDE, SPAN)
            total[span, :] += dot(cellmats[c], values[step, span, :])
        back.wait_recv()
        values[step, pl.ds(end, SIDE), :] = (ghosts[step].astype(F32) * has_next).astype(BF16)
        span = pl.ds(end - STRIDE, SPAN)
        total[span, :] += dot(cellmats[cells - 1], values[step, span, :])
        if step == 0:
            mat_copy.wait_recv()
        ahead.wait_recv()
        shared = dot(behind_mat[:, :STRIDE], behind[step]) + dot(
            behind_mat[:, STRIDE:], values[step, pl.ds(0, SIDE), :]
        )
        total[pl.ds(0, SIDE), :] += shared * has_prev
        own = pl.ds(0, end)
        current = values[step, own, :].astype(F32)
        image = total[own, :] + pots[...] * current
        if step == 0:
            values[1, own, :] = ((image - filter_center * current) / filter_half).astype(BF16)
        elif step < DEGREE:
            previous = values[step - 1, own, :].astype(F32)
            scaled = 2.0 * (image - filter_center * current) / filter_half
            values[step + 1, own, :] = (scaled - previous).astype(BF16)
        else:
            both[:, :width] = values[step, own, :]
            both[:, width:] = image.astype(BF16)

    def give(b, carry):
        part = out_ref.shape[1]
        row = lax.broadcasted_iota(jnp.int32, (part, STRIDE), 0)
        target = jnp.where(row < share, row + b * share, -2)
        found = jnp.zeros((part, 2 * width), F32)
        for c in range(cells):
            pick = equal(ids_row[c, :, pl.ds(0, STRIDE)], target)
            found += dot(pick.astype(BF16), both[pl.ds(c * STRIDE, STRIDE), :])
        out_ref[b] = found.astype(BF16)
        return carry

    lax.fori_loop(0, blocks, give, 0)
    mat_copy.wait_send()
    for copy in copies:
        copy.wait_send()


BLOCK = 256


def project_kernel(
    sizes,
    rows_ref,
    residual_ref,
    projected_ref,
    left,
    right,
    packed,
    from_core,
    for_x,
    from_x,
    for_y,
    from_y,
    for_z,
    from_z,
    final,
    gathered,
    core_sem,
    x_sem,
    y_sem,
    z_sem,
    zg_sem,
    yg_sem,
    xg_sem,
    cg_sem,
):
    share, inverse = sizes
    dom, orb = lax.axis_index("dom"), lax.axis_index("orb")
    y, z_lo = dom // 8, lax.rem(dom, 8)
    x, z_hi, core = orb // 4, lax.rem(orb // 2, 2), lax.rem(orb, 2)
    z = z_hi * 8 + z_lo

    def at_core():
        return {"dom": dom, "orb": orb + 1 - 2 * core}

    def at_x(k):
        return {"dom": dom, "orb": lax.rem(x + k, 4) * 4 + z_hi * 2 + core}

    def at_y(k):
        return {"dom": lax.rem(y + k, 8) * 8 + z_lo, "orb": orb}

    def at_z(k):
        there = lax.rem(z + k, 16)
        return {"dom": y * 8 + lax.rem(there, 8), "orb": x * 4 + (there // 8) * 2 + core}

    barrier = pltpu.get_barrier_semaphore()

    def greet(peer):
        pl.semaphore_signal(barrier, inc=1, device_id=peer, device_id_type=MESH)

    greet(at_core())
    for k in range(1, 4):
        greet(at_x(k))
    for k in range(1, 8):
        greet(at_y(k))
    for k in range(1, 16):
        greet(at_z(k))

    def copy(src, dst, sems, k, peer):
        return pltpu.make_async_remote_copy(
            src_ref=src,
            dst_ref=dst,
            send_sem=sems.at[0, k],
            recv_sem=sems.at[1, k],
            device_id=peer,
            device_id_type=MESH,
        )

    blocks, part, lanes = rows_ref.shape
    lane = lax.broadcasted_iota(jnp.int32, (part, lanes), 1)
    for m in range(blocks // 2):
        a, b = rows_ref[2 * m].astype(F32), rows_ref[2 * m + 1].astype(F32)
        cut = pl.ds(m * lanes, lanes)
        left[:, cut] = jnp.where(lane < lanes // 2, a, pltpu.roll(b, lanes // 2, 1)).astype(BF16)
        right[:, cut] = jnp.where(lane < lanes // 2, pltpu.roll(a, lanes // 2, 1), b).astype(BF16)

    count = left.shape[1] // BLOCK
    pairs = [(i, j) for i in range(count) for j in range(i, count)]
    for p, (i, j) in enumerate(pairs):
        block = lax.dot_general(
            left[:, i * BLOCK : (i + 1) * BLOCK],
            right[:, j * BLOCK : (j + 1) * BLOCK],
            (((0,), (0,)), ((), ())),
            preferred_element_type=F32,
        ).astype(BF16)
        packed[pl.ds((2 * p) * BLOCK, BLOCK), :] = block[:, :128]
        packed[pl.ds((2 * p + 1) * BLOCK, BLOCK), :] = block[:, 128:]
    size = packed.shape[0]
    n2, n8, n64, n1024 = size // 2, size // 8, size // 64, size // 1024

    pl.semaphore_wait(barrier, 26)
    waits = []
    step = copy(
        packed.at[pl.ds(pl.multiple_of((1 - core) * n2, n2), n2)], from_core, core_sem, 0, at_core()
    )
    step.start()
    step.wait_recv()
    waits.append(step)
    mine = packed[pl.ds(pl.multiple_of(core * n2, n2), n2), :].astype(F32)
    for_x[...] = (mine + from_core[...].astype(F32)).astype(BF16)

    steps = []
    for k in range(1, 4):
        there = pl.multiple_of(lax.rem(x + k, 4) * n8, n8)
        steps.append(copy(for_x.at[pl.ds(there, n8)], from_x.at[k - 1], x_sem, k - 1, at_x(k)))
        steps[-1].start()
    tot = for_x[pl.ds(pl.multiple_of(x * n8, n8), n8), :].astype(F32)
    for k in range(1, 4):
        steps[k - 1].wait_recv()
        tot += from_x[k - 1].astype(F32)
    for_y[...] = tot.astype(BF16)
    waits += steps

    steps = []
    for k in range(1, 8):
        there = pl.multiple_of(lax.rem(y + k, 8) * n64, 16)
        steps.append(copy(for_y.at[pl.ds(there, n64)], from_y.at[k - 1], y_sem, k - 1, at_y(k)))
        steps[-1].start()
    tot = for_y[pl.ds(pl.multiple_of(y * n64, 16), n64), :].astype(F32)
    for k in range(1, 8):
        steps[k - 1].wait_recv()
        tot += from_y[k - 1].astype(F32)
    for j in range(16):
        for_z[j] = tot[j * n1024 : (j + 1) * n1024]
    waits += steps

    steps = []
    for k in range(1, 16):
        there = lax.rem(z + k, 16)
        steps.append(copy(for_z.at[there], from_z.at[k - 1], z_sem, k - 1, at_z(k)))
        steps[-1].start()
    tot = for_z[z]
    for k in range(1, 16):
        steps[k - 1].wait_recv()
        tot += from_z[k - 1]
    waits += steps
    final[z] = tot * inverse
    steps = []
    for k in range(1, 16):
        steps.append(copy(final.at[z], final.at[z], zg_sem, k - 1, at_z(k)))
        steps[-1].start()
    for k in range(1, 16):
        steps[k - 1].wait_recv()
    waits += steps

    whole = jnp.concatenate([final[j] for j in range(16)], axis=0).astype(BF16)
    home = pl.ds(pl.multiple_of(((core * 4 + x) * 8 + y) * n64, 16), n64)
    gathered[home, :] = whole
    steps = []
    for k in range(1, 8):
        steps.append(copy(gathered.at[home], gathered.at[home], yg_sem, k - 1, at_y(k)))
        steps[-1].start()
    for k in range(1, 8):
        steps[k - 1].wait_recv()
    waits += steps
    home = pl.ds(pl.multiple_of((core * 4 + x) * n8, n8), n8)
    steps = []
    for k in range(1, 4):
        steps.append(copy(gathered.at[home], gathered.at[home], xg_sem, k - 1, at_x(k)))
        steps[-1].start()
    for k in range(1, 4):
        steps[k - 1].wait_recv()
    waits += steps
    home = pl.ds(pl.multiple_of(core * n2, n2), n2)
    step = copy(gathered.at[home], gathered.at[home], cg_sem, 0, at_core())
    step.start()
    step.wait_recv()
    waits.append(step)

    for p, (i, j) in enumerate(pairs):
        for h in range(2):
            tile = gathered[pl.ds((2 * p + h) * BLOCK, BLOCK), :]
            projected_ref[i * BLOCK : (i + 1) * BLOCK, j * BLOCK + h * 128 : j * BLOCK + (h + 1) * 128] = tile
            if j > i:
                turned = jnp.transpose(tile.astype(F32)).astype(BF16)
                projected_ref[
                    j * BLOCK + h * 128 : j * BLOCK + (h + 1) * 128, i * BLOCK : (i + 1) * BLOCK
                ] = turned
    for j in range(count):
        cut = slice(j * BLOCK, (j + 1) * BLOCK)
        out = right[:, cut].astype(F32) - dot(left[...], projected_ref[:, cut])
        residual_ref[:, cut] = out[:share]
    for step in waits:
        step.wait_send()


def body(orbitals, potential, cell_hamiltonian, connectivity, face_nodes):
    owned, width = orbitals.shape
    cells, npc, _ = cell_hamiltonian.shape
    peers, domains = lax.axis_size("orb"), lax.axis_size("dom")
    share = owned // peers
    part = -(-share // 16) * 16
    end = cells * STRIDE
    upper = lax.reduce_precision(potential, 8, 7)
    rest = potential - upper
    middle = lax.reduce_precision(rest, 8, 7)
    lower = lax.reduce_precision(rest - middle, 8, 7)
    terms = jnp.stack([upper, middle, lower], axis=1).astype(BF16)
    nodes = jnp.concatenate([orbitals, terms, jnp.zeros((owned, 128 - width - 3), BF16)], axis=1)
    vmem = pl.BlockSpec(memory_space=pltpu.VMEM)
    steps = DEGREE + 1
    blocks = pl.pallas_call(
        functools.partial(filter_kernel, (cells, npc, owned, share, peers)),
        out_shape=jax.ShapeDtypeStruct((peers, part, 2 * width), BF16),
        in_specs=[vmem] * 6,
        out_specs=vmem,
        scratch_shapes=[
            pltpu.VMEM((steps, end + SIDE, width), BF16),
            pltpu.VMEM((cells, SPAN, SPAN), BF16),
            pltpu.VMEM((end + SIDE, width), F32),
            pltpu.VMEM((end, width), F32),
            pltpu.VMEM((cells, SPAN, 1), jnp.int32),
            pltpu.VMEM((cells, 1, SPAN), jnp.int32),
            pltpu.VMEM((end, 2 * width), BF16),
            pltpu.VMEM((steps, SIDE, width), BF16),
            pltpu.VMEM((steps, STRIDE, width), BF16),
            pltpu.VMEM((SIDE, SPAN), BF16),
            pltpu.SemaphoreType.DMA((steps, 2)),
            pltpu.SemaphoreType.DMA((steps, 2)),
            pltpu.SemaphoreType.DMA((2,)),
        ],
        compiler_params=pltpu.CompilerParams(
            collective_id=0, has_side_effects=True, vmem_limit_bytes=60 << 20
        ),
        name="chebyshev_filter",
    )(
        nodes,
        cell_hamiltonian,
        connectivity,
        connectivity.T,
        face_nodes[None, :],
        face_nodes[:, None],
    )
    rows = lax.all_to_all(blocks, "orb", split_axis=0, concat_axis=0, tiled=True)
    orbs = peers * width
    count = orbs // BLOCK
    size = count * (count + 1) // 2 * 2 * BLOCK
    residual, projected = pl.pallas_call(
        functools.partial(project_kernel, (share, 1.0 / (owned * domains))),
        out_shape=(
            jax.ShapeDtypeStruct((share, orbs), F32),
            jax.ShapeDtypeStruct((orbs, orbs), BF16),
        ),
        in_specs=[vmem],
        out_specs=(vmem, vmem),
        scratch_shapes=[
            pltpu.VMEM((part, orbs), BF16),
            pltpu.VMEM((part, orbs), BF16),
            pltpu.VMEM((size, 128), BF16),
            pltpu.VMEM((size // 2, 128), BF16),
            pltpu.VMEM((size // 2, 128), BF16),
            pltpu.VMEM((3, size // 8, 128), BF16),
            pltpu.VMEM((size // 8, 128), BF16),
            pltpu.VMEM((7, size // 64, 128), BF16),
            pltpu.VMEM((16, size // 1024, 128), F32),
            pltpu.VMEM((15, size // 1024, 128), F32),
            pltpu.VMEM((16, size // 1024, 128), F32),
            pltpu.VMEM((size, 128), BF16),
            pltpu.SemaphoreType.DMA((2, 1)),
            pltpu.SemaphoreType.DMA((2, 3)),
            pltpu.SemaphoreType.DMA((2, 7)),
            pltpu.SemaphoreType.DMA((2, 15)),
            pltpu.SemaphoreType.DMA((2, 15)),
            pltpu.SemaphoreType.DMA((2, 7)),
            pltpu.SemaphoreType.DMA((2, 3)),
            pltpu.SemaphoreType.DMA((2, 1)),
        ],
        compiler_params=pltpu.CompilerParams(
            collective_id=1, has_side_effects=True, vmem_limit_bytes=60 << 20
        ),
        name="project",
    )(rows)
    return residual, projected


def solution(mesh):
    return jax.shard_map(
        body,
        mesh=mesh,
        in_specs=(P("dom", "orb"), P("dom"), P("dom", None, None), P("dom", None), P("dom")),
        out_specs=(P(("dom", "orb"), None), P()),
        check_vma=False,
    )
```

```python
import functools

import jax
import jax.numpy as jnp
from jax import lax
from jax.experimental import pallas as pl
from jax.experimental.pallas import tpu as pltpu
from jax.sharding import PartitionSpec as P

DEGREE = 4
MESH = pl.DeviceIdType.MESH
F32 = jnp.float32
BF16 = jnp.bfloat16

filter_center = 1.5
filter_half = 2.0

SIDE = 64
STRIDE = 320
SPAN = STRIDE + SIDE


def prefix_tables(n):
    before = lax.broadcasted_iota(jnp.int32, (n, n), 0) < lax.broadcasted_iota(jnp.int32, (n, n), 1)
    after = lax.broadcasted_iota(jnp.int32, (n, n), 0) > lax.broadcasted_iota(jnp.int32, (n, n), 1)
    return before.astype(F32).astype(BF16), after.astype(F32).astype(BF16)


def dot(a, b):
    return jnp.dot(a, b, preferred_element_type=F32)


def equal(a, b):
    return (a == b).astype(F32)


BLOCK = 256


def step_kernel(
    sizes,
    nodes_ref,
    pot_ref,
    mats_ref,
    conn_ref,
    face_ref,
    left_ref,
    right_ref,
    sum_ref,
    table,
    values,
    cellmats,
    total,
    pots,
    ids_col,
    ids_row,
    both,
    ghosts,
    behind,
    behind_mat,
    filtered_out,
    filtered_in,
    image_out,
    image_in,
    packed,
    from_core,
    for_x,
    from_x,
    for_y,
    from_y,
    for_z,
    from_z,
    final,
    gathered,
    halo_sem,
    mat_sem,
    filtered_sem,
    image_sem,
    core_sem,
    x_sem,
    y_sem,
    z_sem,
    zg_sem,
    yg_sem,
    xg_sem,
    cg_sem,
):
    cells, npc, owned, share, inverse = sizes
    dom, orb = lax.axis_index("dom"), lax.axis_index("orb")
    domains = lax.axis_size("dom")
    y, z_lo = dom // 8, lax.rem(dom, 8)
    x, z_hi, core = orb // 4, lax.rem(orb // 2, 2), lax.rem(orb, 2)
    z = z_hi * 8 + z_lo
    nxt = {"dom": lax.rem(dom + 1, domains), "orb": orb}
    prv = {"dom": lax.rem(dom + domains - 1, domains), "orb": orb}

    def at_core():
        return {"dom": dom, "orb": orb + 1 - 2 * core}

    def at_x(k):
        return {"dom": dom, "orb": lax.rem(x + k, 4) * 4 + z_hi * 2 + core}

    def at_y(k):
        return {"dom": lax.rem(y + k, 8) * 8 + z_lo, "orb": orb}

    def at_z(k):
        there = lax.rem(z + k, 16)
        return {"dom": y * 8 + lax.rem(there, 8), "orb": x * 4 + (there // 8) * 2 + core}

    def orb_at(k):
        return (
            lax.rem(x + k // 4, 4) * 4 + lax.rem(z_hi + k // 2 % 2, 2) * 2 + lax.rem(core + k % 2, 2)
        )

    far_first = [k for k in range(1, 16) if k // 2 % 2] + [k for k in range(1, 16) if not k // 2 % 2]

    def copy(src, dst, sems, k, peer):
        return pltpu.make_async_remote_copy(
            src_ref=src,
            dst_ref=dst,
            send_sem=sems.at[0, k],
            recv_sem=sems.at[1, k],
            device_id=peer,
            device_id_type=MESH,
        )

    barrier = pltpu.get_barrier_semaphore()
    peers = [prv, nxt, at_core()]
    peers += [at_x(k) for k in range(1, 4)]
    peers += [at_y(k) for k in range(1, 8)]
    peers += [at_z(k) for k in range(1, 16)]
    peers += [{"dom": dom, "orb": orb_at(k)} for k in range(1, 16)]
    for peer in peers:
        pl.semaphore_signal(barrier, inc=1, device_id=peer, device_id_type=MESH)

    width = values.shape[2]
    pot = pot_ref[...]
    upper = pot.astype(BF16)
    rest = pot - upper.astype(F32)
    middle = rest.astype(BF16)
    lower = (rest - middle.astype(F32)).astype(BF16)
    table[pl.ds(0, width), :] = nodes_ref[...]
    place = lax.broadcasted_iota(jnp.int32, (16, owned), 0)
    terms = jnp.where(
        place == 0,
        upper.astype(F32),
        jnp.where(place == 1, middle.astype(F32), jnp.where(place == 2, lower.astype(F32), 0.0)),
    )
    table[pl.ds(width, 16), :] = terms.astype(BF16)

    conn = conn_ref[...].astype(F32)
    turned = jnp.transpose(conn)
    rows = [conn[c : c + 1, :] for c in range(cells)]
    cols = [turned[:, c : c + 1] for c in range(cells)]
    face_row = face_ref[...].astype(F32)
    face_col = jnp.transpose(jnp.broadcast_to(face_row, (8, face_row.shape[1])))[:, :1]
    faces = face_row.shape[1]

    low = [equal(cols[c], rows[c + 1]) for c in range(cells - 1)]
    high = [equal(cols[c + 1], rows[c]) for c in range(cells - 1)]
    first_row = equal(face_col, rows[0])
    first_col = equal(cols[0], face_row)
    bottom_row = [jnp.sum(first_row, axis=0, keepdims=True)]
    bottom_row += [jnp.sum(low[c], axis=0, keepdims=True) for c in range(cells - 1)]
    bottom_col = [jnp.sum(first_col, axis=1, keepdims=True)]
    bottom_col += [jnp.sum(high[c], axis=1, keepdims=True) for c in range(cells - 1)]
    top_row = [jnp.sum(high[c], axis=0, keepdims=True) for c in range(cells - 1)]
    top_row += [(rows[-1] >= owned).astype(F32)]
    top_col = [jnp.sum(low[c], axis=1, keepdims=True) for c in range(cells - 1)]
    top_col += [(cols[-1] >= owned).astype(F32)]

    before, after = prefix_tables(npc)
    inner_row = [1.0 - bottom_row[c] - top_row[c] for c in range(cells)]
    inner_col = [1.0 - bottom_col[c] - top_col[c] for c in range(cells)]
    stacked_row = jnp.concatenate(bottom_row + inner_row, axis=0).astype(BF16)
    stacked_col = jnp.concatenate(bottom_col + inner_col, axis=1).astype(BF16)
    rank_row = dot(stacked_row, before)
    rank_col = dot(after, stacked_col)
    place_row = lax.broadcasted_iota(jnp.int32, (faces, 1), 0).astype(F32)
    place_col = lax.broadcasted_iota(jnp.int32, (1, faces), 1).astype(F32)
    low_row = [jnp.sum(first_row * place_row, axis=0, keepdims=True)]
    low_row += [rank_row[c : c + 1] for c in range(1, cells)]
    low_col = [jnp.sum(first_col * place_col, axis=1, keepdims=True)]
    low_col += [rank_col[:, c : c + 1] for c in range(1, cells)]
    high_row = [jnp.sum(high[c] * low_col[c + 1], axis=0, keepdims=True) for c in range(cells - 1)]
    high_row += [rows[-1] - owned]
    high_col = [jnp.sum(low[c] * low_row[c + 1], axis=1, keepdims=True) for c in range(cells - 1)]
    high_col += [cols[-1] - owned]

    def slots(bottom, top, low_rank, high_rank, inner_rank):
        inner = SIDE + inner_rank
        return jnp.where(bottom > 0.5, low_rank, jnp.where(top > 0.5, STRIDE + high_rank, inner)).astype(
            jnp.int32
        )

    def spread_of(c):
        slot_row = slots(
            bottom_row[c], top_row[c], low_row[c], high_row[c], rank_row[cells + c : cells + c + 1]
        )
        slot_col = slots(
            bottom_col[c], top_col[c], low_col[c], high_col[c], rank_col[:, cells + c : cells + c + 1]
        )
        down = equal(lax.broadcasted_iota(jnp.int32, (SPAN, npc), 0), slot_row)
        across = equal(slot_col, lax.broadcasted_iota(jnp.int32, (npc, SPAN), 1))
        return down, across

    order = [cells - 1] + list(range(cells - 1))
    for c in order:
        down, across = spread_of(c)
        named = rows[c] + 1.0
        ids_col[c] = (jnp.sum(down * named, axis=1, keepdims=True) - 1.0).astype(jnp.int32)
        named = cols[c] + 1.0
        ids_row[c] = (jnp.sum(across * named, axis=0, keepdims=True) - 1.0).astype(jnp.int32)
        half = dot(down.astype(BF16), mats_ref[c]).astype(BF16)
        cellmats[c] = dot(half, across.astype(BF16)).astype(BF16)

    pl.semaphore_wait(barrier, len(peers))
    waits = []
    mat_copy = copy(cellmats.at[cells - 1, pl.ds(STRIDE, SIDE)], behind_mat, mat_sem, 0, nxt)
    mat_copy.start()
    waits.append(mat_copy)

    def take(c, carry):
        pick = equal(
            ids_col[c, pl.ds(0, STRIDE), :], lax.broadcasted_iota(jnp.int32, (STRIDE, owned), 1)
        )
        found = lax.dot_general(
            pick.astype(BF16), table[...], (((1,), (1,)), ((), ())), preferred_element_type=F32
        )
        start = pl.multiple_of(c * STRIDE, STRIDE)
        values[0, pl.ds(start, STRIDE), :] = found[:, :width].astype(BF16)
        pot = found[:, width : width + 1] + found[:, width + 1 : width + 2] + found[:, width + 2 : width + 3]
        pots[pl.ds(start, STRIDE), :] = jnp.broadcast_to(pot, (STRIDE, width))
        return carry

    lax.fori_loop(0, cells, take, 0)

    part = filtered_out.shape[1]
    padded = left_ref.shape[0] // 2

    def give(out):
        def one(b, carry):
            row = lax.broadcasted_iota(jnp.int32, (2 * padded, STRIDE), 0)
            low = jnp.where(row < part, row, -2 - owned)
            high = jnp.where(row < padded + share - part, row - padded + part, -2 - owned)
            target = jnp.where(row < padded, low, high) + b * share
            found = jnp.zeros((2 * padded, 2 * width), F32)
            for c in range(cells):
                pick = equal(ids_row[c, :, pl.ds(0, STRIDE)], target)
                found += dot(pick.astype(BF16), both[pl.ds(c * STRIDE, STRIDE), :])
            lane = lax.broadcasted_iota(jnp.int32, (padded, 2 * width), 1)
            out[b] = jnp.where(lane < width, found[:padded], found[padded:])[:part].astype(BF16)
            return carry

        lax.fori_loop(0, 16, one, 0)

    def exchange(out, into, sems):
        steps = {}
        for k in far_first:
            there = orb_at(k)
            steps[k] = copy(out.at[there], into.at[orb], sems, k - 1, {"dom": dom, "orb": there})
            steps[k].start()
        into[orb] = out[orb]
        return [steps[k] for k in range(1, 16)]

    end = cells * STRIDE
    has_next = (dom < domains - 1).astype(F32)
    has_prev = (dom > 0).astype(F32)
    for step in range(DEGREE + 1):
        back = copy(values.at[step, pl.ds(0, SIDE)], ghosts.at[step], halo_sem, 2 * step, prv)
        ahead = copy(
            values.at[step, pl.ds(end - STRIDE, STRIDE)], behind.at[step], halo_sem, 2 * step + 1, nxt
        )
        back.start()
        ahead.start()
        waits += [back, ahead]
        own = pl.ds(0, end)
        if step == DEGREE:
            both[:, :width] = values[step, own, :]
            both[:, width:] = values[step, own, :]
            give(filtered_out)
            filtered_steps = exchange(filtered_out, filtered_in, filtered_sem)
        total[...] = jnp.zeros_like(total)
        for c in range(cells - 1):
            span = pl.ds(c * STRIDE, SPAN)
            total[span, :] += dot(cellmats[c], values[step, span, :])
        back.wait_recv()
        values[step, pl.ds(end, SIDE), :] = (ghosts[step].astype(F32) * has_next).astype(BF16)
        span = pl.ds(end - STRIDE, SPAN)
        total[span, :] += dot(cellmats[cells - 1], values[step, span, :])
        if step == 0:
            mat_copy.wait_recv()
        ahead.wait_recv()
        shared = dot(behind_mat[:, :STRIDE], behind[step]) + dot(
            behind_mat[:, STRIDE:], values[step, pl.ds(0, SIDE), :]
        )
        total[pl.ds(0, SIDE), :] += shared * has_prev
        current = values[step, own, :].astype(F32)
        image = total[own, :] + pots[...] * current
        if step == 0:
            values[1, own, :] = ((image - filter_center * current) / filter_half).astype(BF16)
        elif step < DEGREE:
            previous = values[step - 1, own, :].astype(F32)
            scaled = 2.0 * (image - filter_center * current) / filter_half
            values[step + 1, own, :] = (scaled - previous).astype(BF16)
        else:
            both[:, :width] = image.astype(BF16)
            both[:, width:] = image.astype(BF16)
    give(image_out)
    image_steps = exchange(image_out, image_in, image_sem)
    waits += filtered_steps + image_steps

    lanes = 2 * width
    lane = lax.broadcasted_iota(jnp.int32, (part, lanes), 1)

    def assemble(into, out):
        out[...] = jnp.zeros_like(out)
        for m in range(8):
            a, b = into[2 * m].astype(F32), into[2 * m + 1].astype(F32)
            cut = pl.ds(m * lanes, lanes)
            low = jnp.where(lane < width, a, pltpu.roll(b, width, 1))
            high = jnp.where(lane < width, pltpu.roll(a, width, 1), b)
            out[pl.ds(0, part), cut] = low.astype(BF16)
            out[pl.ds(padded, part), cut] = high.astype(BF16)

    for step in filtered_steps:
        step.wait_recv()
    assemble(filtered_in, left_ref)
    for step in image_steps:
        step.wait_recv()
    assemble(image_in, right_ref)

    count = left_ref.shape[1] // BLOCK
    pairs = [(i, j) for i in range(count) for j in range(i, count)]
    for p, (i, j) in enumerate(pairs):
        block = lax.dot_general(
            left_ref[:, i * BLOCK : (i + 1) * BLOCK],
            right_ref[:, j * BLOCK : (j + 1) * BLOCK],
            (((0,), (0,)), ((), ())),
            preferred_element_type=F32,
        ).astype(BF16)
        packed[pl.ds((2 * p) * BLOCK, BLOCK), :] = block[:, :128]
        packed[pl.ds((2 * p + 1) * BLOCK, BLOCK), :] = block[:, 128:]
    size = packed.shape[0]
    n2, n8, n64, n1024 = size // 2, size // 8, size // 64, size // 1024

    def at(piece, rows):
        return pl.ds(pl.multiple_of(piece * rows, 16), rows)

    order = (1, 3, 2, 0)
    steps = {}
    for k in order:
        piece = (1 - core) * 4 + lax.rem(x + k, 4)
        steps[k] = copy(packed.at[at(piece, n8)], from_core.at[k], core_sem, k, at_core())
        steps[k].start()
    waits += [steps[k] for k in order]
    x_steps = {}
    for k in order:
        steps[k].wait_recv()
        mine = packed[at(core * 4 + lax.rem(x + k, 4), n8), :].astype(F32) + from_core[k].astype(F32)
        if k:
            for_x[k] = mine.astype(BF16)
            x_steps[k] = copy(for_x.at[k], from_x.at[k - 1], x_sem, k - 1, at_x(k))
            x_steps[k].start()
    waits += [x_steps[k] for k in range(1, 4)]
    tot = mine
    for k in range(1, 4):
        x_steps[k].wait_recv()
        tot += from_x[k - 1].astype(F32)
    for_y[...] = tot.astype(BF16)

    steps = {}
    for k in (4, 3, 5, 2, 6, 1, 7):
        steps[k] = copy(for_y.at[at(lax.rem(y + k, 8), n64)], from_y.at[k - 1], y_sem, k - 1, at_y(k))
        steps[k].start()
    tot = for_y[at(y, n64), :].astype(F32)
    for k in (1, 7, 2, 6, 3, 5, 4):
        steps[k].wait_recv()
        tot += from_y[k - 1].astype(F32)
        waits.append(steps[k])
    for j in range(16):
        for_z[j] = tot[j * n1024 : (j + 1) * n1024]

    steps = {}
    spread = [8, 7, 9, 6, 10, 5, 11, 4, 12, 3, 13, 2, 14, 1, 15]
    for k in spread:
        there = lax.rem(z + k, 16)
        steps[k] = copy(for_z.at[there], from_z.at[k - 1], z_sem, k - 1, at_z(k))
        steps[k].start()
    tot = for_z[z]
    for k in reversed(spread):
        steps[k].wait_recv()
        tot += from_z[k - 1]
        waits.append(steps[k])
    final[z] = tot * inverse
    steps = {}
    for k in spread:
        steps[k] = copy(final.at[z], final.at[z], zg_sem, k - 1, at_z(k))
        steps[k].start()
    for k in reversed(spread):
        steps[k].wait_recv()
        waits.append(steps[k])

    whole = jnp.concatenate([final[j] for j in range(16)], axis=0).astype(BF16)
    group = core * 4 + x
    home = at(group * 8 + y, n64)
    gathered[home, :] = whole
    y_steps = {}
    for k in (4, 3, 5, 2, 6, 1, 7):
        y_steps[k] = copy(gathered.at[home], gathered.at[home], yg_sem, k - 1, at_y(k))
        y_steps[k].start()
    x_steps = {}
    for r in (0, 1, 7, 2, 6, 3, 5, 4):
        if r:
            y_steps[r].wait_recv()
            waits.append(y_steps[r])
        spot = at(group * 8 + lax.rem(y + 8 - r, 8), n64)
        for k in (2, 1, 3):
            x_steps[k, r] = copy(gathered.at[spot], gathered.at[spot], xg_sem, (k - 1) * 8 + r, at_x(k))
            x_steps[k, r].start()
    core_steps = {}
    for k in (0, 1, 3, 2):
        if k:
            for r in (0, 1, 7, 2, 6, 3, 5, 4):
                x_steps[k, r].wait_recv()
                waits.append(x_steps[k, r])
        spot = at(core * 4 + lax.rem(x + 4 - k, 4), n8)
        core_steps[k] = copy(gathered.at[spot], gathered.at[spot], cg_sem, k, at_core())
        core_steps[k].start()
    for k in (0, 1, 3, 2):
        core_steps[k].wait_recv()
        waits.append(core_steps[k])
    sum_ref[...] = gathered[...]
    for step in waits:
        step.wait_send()


def residual_kernel(left_ref, right_ref, sum_ref, residual_ref, projected_ref):
    share = residual_ref.shape[0]
    padded = left_ref.shape[0] // 2
    part = (share + 1) // 2
    count = left_ref.shape[1] // BLOCK
    pairs = [(i, j) for i in range(count) for j in range(i, count)]
    for p, (i, j) in enumerate(pairs):
        for h in range(2):
            tile = sum_ref[pl.ds((2 * p + h) * BLOCK, BLOCK), :]
            start = j * BLOCK + h * 128
            projected_ref[i * BLOCK : (i + 1) * BLOCK, start : start + 128] = tile
            if j > i:
                turned = jnp.transpose(tile.astype(F32)).astype(BF16)
                projected_ref[start : start + 128, i * BLOCK : (i + 1) * BLOCK] = turned
    for j in range(count):
        cut = slice(j * BLOCK, (j + 1) * BLOCK)
        out = right_ref[:, cut].astype(F32) - dot(left_ref[...], projected_ref[:, cut])
        residual_ref[:part, cut] = out[:part]
        residual_ref[part:, cut] = out[padded : padded + share - part]


def body(orbitals, potential, cell_hamiltonian, connectivity, face_nodes):
    owned, width = orbitals.shape
    cells, npc, _ = cell_hamiltonian.shape
    peers, domains = lax.axis_size("orb"), lax.axis_size("dom")
    share = owned // peers
    part = (share + 1) // 2
    padded = -(-part // 16) * 16
    end = cells * STRIDE
    orbs = peers * width
    count = orbs // BLOCK
    size = count * (count + 1) // 2 * 2 * BLOCK
    vmem = pl.BlockSpec(memory_space=pltpu.VMEM)
    steps = DEGREE + 1
    sem = pltpu.SemaphoreType.DMA
    left, right, sums = pl.pallas_call(
        functools.partial(step_kernel, (cells, npc, owned, share, 1.0 / (owned * domains))),
        out_shape=(
            jax.ShapeDtypeStruct((2 * padded, orbs), BF16),
            jax.ShapeDtypeStruct((2 * padded, orbs), BF16),
            jax.ShapeDtypeStruct((size, 128), BF16),
        ),
        in_specs=[vmem] * 5,
        out_specs=(vmem,) * 3,
        scratch_shapes=[
            pltpu.VMEM((width + 16, owned), BF16),
            pltpu.VMEM((steps, end + SIDE, width), BF16),
            pltpu.VMEM((cells, SPAN, SPAN), BF16),
            pltpu.VMEM((end + SIDE, width), F32),
            pltpu.VMEM((end, width), F32),
            pltpu.VMEM((cells, SPAN, 1), jnp.int32),
            pltpu.VMEM((cells, 1, SPAN), jnp.int32),
            pltpu.VMEM((end, 2 * width), BF16),
            pltpu.VMEM((steps, SIDE, width), BF16),
            pltpu.VMEM((steps, STRIDE, width), BF16),
            pltpu.VMEM((SIDE, SPAN), BF16),
            pltpu.VMEM((peers, part, 2 * width), BF16),
            pltpu.VMEM((peers, part, 2 * width), BF16),
            pltpu.VMEM((peers, part, 2 * width), BF16),
            pltpu.VMEM((peers, part, 2 * width), BF16),
            pltpu.VMEM((size, 128), BF16),
            pltpu.VMEM((4, size // 8, 128), BF16),
            pltpu.VMEM((4, size // 8, 128), BF16),
            pltpu.VMEM((3, size // 8, 128), BF16),
            pltpu.VMEM((size // 8, 128), BF16),
            pltpu.VMEM((7, size // 64, 128), BF16),
            pltpu.VMEM((16, size // 1024, 128), F32),
            pltpu.VMEM((15, size // 1024, 128), F32),
            pltpu.VMEM((16, size // 1024, 128), F32),
            pltpu.VMEM((size, 128), BF16),
            sem((2, 2 * steps)),
            sem((2, 1)),
            sem((2, 15)),
            sem((2, 15)),
            sem((2, 4)),
            sem((2, 3)),
            sem((2, 7)),
            sem((2, 15)),
            sem((2, 15)),
            sem((2, 7)),
            sem((2, 24)),
            sem((2, 4)),
        ],
        compiler_params=pltpu.CompilerParams(
            collective_id=0, has_side_effects=True, vmem_limit_bytes=60 << 20
        ),
        name="filter_and_project",
    )(orbitals.T, potential[None, :], cell_hamiltonian, connectivity, face_nodes[None, :])
    return pl.pallas_call(
        residual_kernel,
        out_shape=(
            jax.ShapeDtypeStruct((share, orbs), F32),
            jax.ShapeDtypeStruct((orbs, orbs), BF16),
        ),
        in_specs=[vmem] * 3,
        out_specs=(vmem, vmem),
        compiler_params=pltpu.CompilerParams(vmem_limit_bytes=60 << 20),
        name="residual",
    )(left, right, sums)


def solution(mesh):
    return jax.shard_map(
        body,
        mesh=mesh,
        in_specs=(P("dom", "orb"), P("dom"), P("dom", None, None), P("dom", None), P("dom")),
        out_specs=(P(("dom", "orb"), None), P()),
        check_vma=False,
    )
```

```python
import functools

import jax
import jax.numpy as jnp
from jax import lax
from jax.experimental import pallas as pl
from jax.experimental.pallas import tpu as pltpu
from jax.sharding import PartitionSpec as P

DEGREE = 4
MESH = pl.DeviceIdType.MESH
F32 = jnp.float32
BF16 = jnp.bfloat16

filter_center = 1.5
filter_half = 2.0

SIDE = 64
STRIDE = 320
SPAN = STRIDE + SIDE


def prefix_tables(n):
    before = lax.broadcasted_iota(jnp.int32, (n, n), 0) < lax.broadcasted_iota(jnp.int32, (n, n), 1)
    after = lax.broadcasted_iota(jnp.int32, (n, n), 0) > lax.broadcasted_iota(jnp.int32, (n, n), 1)
    return before.astype(F32).astype(BF16), after.astype(F32).astype(BF16)


def dot(a, b):
    return jnp.dot(a, b, preferred_element_type=F32)


def equal(a, b):
    return (a == b).astype(F32)


BLOCK = 256


def step_kernel(
    sizes,
    nodes_ref,
    pot_ref,
    mats_ref,
    conn_ref,
    face_ref,
    left_ref,
    right_ref,
    sum_ref,
    table,
    values,
    cellmats,
    total,
    pots,
    ids_col,
    ids_row,
    both,
    ghosts,
    behind,
    behind_mat,
    filtered_out,
    filtered_in,
    image_out,
    image_in,
    packed,
    from_core,
    for_x,
    from_x,
    for_y,
    from_y,
    for_z,
    from_z,
    final,
    gathered,
    halo_sem,
    mat_sem,
    filtered_sem,
    image_sem,
    core_sem,
    x_sem,
    y_sem,
    z_sem,
    zg_sem,
    yg_sem,
    xg_sem,
    cg_sem,
):
    cells, npc, owned, share, inverse = sizes
    dom, orb = lax.axis_index("dom"), lax.axis_index("orb")
    domains = lax.axis_size("dom")
    y, z_lo = dom // 8, lax.rem(dom, 8)
    x, z_hi, core = orb // 4, lax.rem(orb // 2, 2), lax.rem(orb, 2)
    z = z_hi * 8 + z_lo
    nxt = {"dom": lax.rem(dom + 1, domains), "orb": orb}
    prv = {"dom": lax.rem(dom + domains - 1, domains), "orb": orb}

    def at_core():
        return {"dom": dom, "orb": orb + 1 - 2 * core}

    def at_x(k):
        return {"dom": dom, "orb": lax.rem(x + k, 4) * 4 + z_hi * 2 + core}

    def at_y(k):
        return {"dom": lax.rem(y + k, 8) * 8 + z_lo, "orb": orb}

    def at_z(k):
        there = lax.rem(z + k, 16)
        return {"dom": y * 8 + lax.rem(there, 8), "orb": x * 4 + (there // 8) * 2 + core}

    def orb_at(v):
        u = lax.rem(v, 8)
        return (
            lax.rem(x + u // 2, 4) * 4 + lax.rem(z_hi + 1 - v // 8, 2) * 2 + lax.rem(core + lax.rem(u, 2), 2)
        )

    others = [v for v in range(16) if v != 8]

    def copy(src, dst, sems, k, peer):
        return pltpu.make_async_remote_copy(
            src_ref=src,
            dst_ref=dst,
            send_sem=sems.at[0, k],
            recv_sem=sems.at[1, k],
            device_id=peer,
            device_id_type=MESH,
        )

    barrier = pltpu.get_barrier_semaphore()
    peers = [prv, nxt, at_core()]
    peers += [at_x(k) for k in range(1, 4)]
    peers += [at_y(k) for k in range(1, 8)]
    peers += [at_z(k) for k in range(1, 16)]
    peers += [{"dom": dom, "orb": orb_at(v)} for v in others]
    for peer in peers:
        pl.semaphore_signal(barrier, inc=1, device_id=peer, device_id_type=MESH)

    width = values.shape[2]
    pot = pot_ref[...]
    upper = pot.astype(BF16)
    rest = pot - upper.astype(F32)
    middle = rest.astype(BF16)
    lower = (rest - middle.astype(F32)).astype(BF16)
    table[pl.ds(0, width), :] = nodes_ref[...]
    place = lax.broadcasted_iota(jnp.int32, (16, owned), 0)
    terms = jnp.where(
        place == 0,
        upper.astype(F32),
        jnp.where(place == 1, middle.astype(F32), jnp.where(place == 2, lower.astype(F32), 0.0)),
    )
    table[pl.ds(width, 16), :] = terms.astype(BF16)

    conn = conn_ref[...].astype(F32)
    turned = jnp.transpose(conn)
    rows = [conn[c : c + 1, :] for c in range(cells)]
    cols = [turned[:, c : c + 1] for c in range(cells)]
    face_row = face_ref[...].astype(F32)
    face_col = jnp.transpose(jnp.broadcast_to(face_row, (8, face_row.shape[1])))[:, :1]
    faces = face_row.shape[1]

    low = [equal(cols[c], rows[c + 1]) for c in range(cells - 1)]
    high = [equal(cols[c + 1], rows[c]) for c in range(cells - 1)]
    first_row = equal(face_col, rows[0])
    first_col = equal(cols[0], face_row)
    bottom_row = [jnp.sum(first_row, axis=0, keepdims=True)]
    bottom_row += [jnp.sum(low[c], axis=0, keepdims=True) for c in range(cells - 1)]
    bottom_col = [jnp.sum(first_col, axis=1, keepdims=True)]
    bottom_col += [jnp.sum(high[c], axis=1, keepdims=True) for c in range(cells - 1)]
    top_row = [jnp.sum(high[c], axis=0, keepdims=True) for c in range(cells - 1)]
    top_row += [(rows[-1] >= owned).astype(F32)]
    top_col = [jnp.sum(low[c], axis=1, keepdims=True) for c in range(cells - 1)]
    top_col += [(cols[-1] >= owned).astype(F32)]

    before, after = prefix_tables(npc)
    inner_row = [1.0 - bottom_row[c] - top_row[c] for c in range(cells)]
    inner_col = [1.0 - bottom_col[c] - top_col[c] for c in range(cells)]
    stacked_row = jnp.concatenate(bottom_row + inner_row, axis=0).astype(BF16)
    stacked_col = jnp.concatenate(bottom_col + inner_col, axis=1).astype(BF16)
    rank_row = dot(stacked_row, before)
    rank_col = dot(after, stacked_col)
    place_row = lax.broadcasted_iota(jnp.int32, (faces, 1), 0).astype(F32)
    place_col = lax.broadcasted_iota(jnp.int32, (1, faces), 1).astype(F32)
    low_row = [jnp.sum(first_row * place_row, axis=0, keepdims=True)]
    low_row += [rank_row[c : c + 1] for c in range(1, cells)]
    low_col = [jnp.sum(first_col * place_col, axis=1, keepdims=True)]
    low_col += [rank_col[:, c : c + 1] for c in range(1, cells)]
    high_row = [jnp.sum(high[c] * low_col[c + 1], axis=0, keepdims=True) for c in range(cells - 1)]
    high_row += [rows[-1] - owned]
    high_col = [jnp.sum(low[c] * low_row[c + 1], axis=1, keepdims=True) for c in range(cells - 1)]
    high_col += [cols[-1] - owned]

    def slots(bottom, top, low_rank, high_rank, inner_rank):
        inner = SIDE + inner_rank
        return jnp.where(bottom > 0.5, low_rank, jnp.where(top > 0.5, STRIDE + high_rank, inner)).astype(
            jnp.int32
        )

    def spread_of(c):
        slot_row = slots(
            bottom_row[c], top_row[c], low_row[c], high_row[c], rank_row[cells + c : cells + c + 1]
        )
        slot_col = slots(
            bottom_col[c], top_col[c], low_col[c], high_col[c], rank_col[:, cells + c : cells + c + 1]
        )
        down = equal(lax.broadcasted_iota(jnp.int32, (SPAN, npc), 0), slot_row)
        across = equal(slot_col, lax.broadcasted_iota(jnp.int32, (npc, SPAN), 1))
        return down, across

    def place_cell(c):
        down, across = spread_of(c)
        named = rows[c] + 1.0
        ids_col[c] = (jnp.sum(down * named, axis=1, keepdims=True) - 1.0).astype(jnp.int32)
        named = cols[c] + 1.0
        ids_row[c] = (jnp.sum(across * named, axis=0, keepdims=True) - 1.0).astype(jnp.int32)
        half = dot(down.astype(BF16), mats_ref[c]).astype(BF16)
        cellmats[c] = dot(half, across.astype(BF16)).astype(BF16)

    def take(c, carry):
        pick = equal(
            ids_col[c, pl.ds(0, STRIDE), :], lax.broadcasted_iota(jnp.int32, (STRIDE, owned), 1)
        )
        found = lax.dot_general(
            pick.astype(BF16), table[...], (((1,), (1,)), ((), ())), preferred_element_type=F32
        )
        start = pl.multiple_of(c * STRIDE, STRIDE)
        values[0, pl.ds(start, STRIDE), :] = found[:, :width].astype(BF16)
        pot = found[:, width : width + 1] + found[:, width + 1 : width + 2] + found[:, width + 2 : width + 3]
        pots[pl.ds(start, STRIDE), :] = jnp.broadcast_to(pot, (STRIDE, width))
        return carry

    end = cells * STRIDE
    waits = []

    def send(step):
        back = copy(values.at[step, pl.ds(0, SIDE)], ghosts.at[step], halo_sem, 2 * step, prv)
        ahead = copy(
            values.at[step, pl.ds(end - STRIDE, STRIDE)], behind.at[step], halo_sem, 2 * step + 1, nxt
        )
        back.start()
        ahead.start()
        waits.extend([back, ahead])
        return back, ahead

    for c in (cells - 1, 0):
        place_cell(c)
        lax.fori_loop(c, c + 1, take, 0)
    pl.semaphore_wait(barrier, len(peers))
    back, ahead = send(0)
    mat_copy = copy(cellmats.at[cells - 1, pl.ds(STRIDE, SIDE)], behind_mat, mat_sem, 0, nxt)
    mat_copy.start()
    waits.append(mat_copy)
    for c in range(1, cells - 1):
        place_cell(c)
    lax.fori_loop(1, cells - 1, take, 0)

    part = filtered_out.shape[1]
    padded = left_ref.shape[0] // 2

    def block_of(b):
        row = lax.broadcasted_iota(jnp.int32, (2 * padded, STRIDE), 0)
        low = jnp.where(row < part, row, -2 - owned)
        high = jnp.where(row < padded + share - part, row - padded + part, -2 - owned)
        target = jnp.where(row < padded, low, high) + b * share
        found = jnp.zeros((2 * padded, 2 * width), F32)
        for c in range(cells):
            pick = equal(ids_row[c, :, pl.ds(0, STRIDE)], target)
            found += dot(pick.astype(BF16), both[pl.ds(c * STRIDE, STRIDE), :])
        lane = lax.broadcasted_iota(jnp.int32, (padded, 2 * width), 1)
        return jnp.where(lane < width, found[:padded], found[padded:])[:part].astype(BF16)

    def exchange(out, into, sems):
        def one_of(v):
            there = orb_at(v)
            return copy(out.at[there], into.at[orb], sems, v, {"dom": dom, "orb": there})

        def one(v, carry):
            there = orb_at(v)
            out[there] = block_of(there)

            @pl.when(v != 0)
            def _():
                one_of(v - 1 - (v == 9).astype(jnp.int32)).start()

            return carry

        lax.fori_loop(0, 8, one, 0)
        lax.fori_loop(9, 16, one, 0)
        into[orb] = block_of(orb)
        one_of(15).start()
        return [one_of(v) for v in others]

    has_next = (dom < domains - 1).astype(F32)
    has_prev = (dom > 0).astype(F32)
    edges = [pl.ds(0, SIDE), pl.ds(end - STRIDE, STRIDE)]
    middle_rows = pl.ds(SIDE, end - STRIDE - SIDE)

    def update(step, some):
        current = values[step, some, :].astype(F32)
        image = total[some, :] + pots[some, :] * current
        if step == 0:
            values[1, some, :] = ((image - filter_center * current) / filter_half).astype(BF16)
        elif step < DEGREE:
            previous = values[step - 1, some, :].astype(F32)
            scaled = 2.0 * (image - filter_center * current) / filter_half
            values[step + 1, some, :] = (scaled - previous).astype(BF16)
        else:
            both[some, :width] = image.astype(BF16)
            both[some, width:] = image.astype(BF16)

    for step in range(DEGREE + 1):
        if step == DEGREE:
            own = pl.ds(0, end)
            both[:, :width] = values[step, own, :]
            both[:, width:] = values[step, own, :]
            filtered_steps = exchange(filtered_out, filtered_in, filtered_sem)
        total[...] = jnp.zeros_like(total)
        for c in range(cells - 1):
            span = pl.ds(c * STRIDE, SPAN)
            total[span, :] += dot(cellmats[c], values[step, span, :])
        update(step, middle_rows)
        back.wait_recv()
        values[step, pl.ds(end, SIDE), :] = (ghosts[step].astype(F32) * has_next).astype(BF16)
        span = pl.ds(end - STRIDE, SPAN)
        total[span, :] += dot(cellmats[cells - 1], values[step, span, :])
        if step == 0:
            mat_copy.wait_recv()
        ahead.wait_recv()
        shared = dot(behind_mat[:, :STRIDE], behind[step]) + dot(
            behind_mat[:, STRIDE:], values[step, pl.ds(0, SIDE), :]
        )
        total[pl.ds(0, SIDE), :] += shared * has_prev
        for some in edges:
            update(step, some)
        if step < DEGREE:
            back, ahead = send(step + 1)
    image_steps = exchange(image_out, image_in, image_sem)
    waits += filtered_steps + image_steps

    lanes = 2 * width
    lane = lax.broadcasted_iota(jnp.int32, (part, lanes), 1)

    def assemble(into, out):
        out[...] = jnp.zeros_like(out)
        for m in range(8):
            a, b = into[2 * m].astype(F32), into[2 * m + 1].astype(F32)
            cut = pl.ds(m * lanes, lanes)
            low = jnp.where(lane < width, a, pltpu.roll(b, width, 1))
            high = jnp.where(lane < width, pltpu.roll(a, width, 1), b)
            out[pl.ds(0, part), cut] = low.astype(BF16)
            out[pl.ds(padded, part), cut] = high.astype(BF16)

    for step in filtered_steps:
        step.wait_recv()
    assemble(filtered_in, left_ref)
    for step in image_steps:
        step.wait_recv()
    assemble(image_in, right_ref)

    count = left_ref.shape[1] // BLOCK
    pairs = [(i, j) for i in range(count) for j in range(i, count)]
    for p, (i, j) in enumerate(pairs):
        block = lax.dot_general(
            left_ref[:, i * BLOCK : (i + 1) * BLOCK],
            right_ref[:, j * BLOCK : (j + 1) * BLOCK],
            (((0,), (0,)), ((), ())),
            preferred_element_type=F32,
        ).astype(BF16)
        packed[pl.ds((2 * p) * BLOCK, BLOCK), :] = block[:, :128]
        packed[pl.ds((2 * p + 1) * BLOCK, BLOCK), :] = block[:, 128:]
    size = packed.shape[0]
    n2, n8, n64, n1024 = size // 2, size // 8, size // 64, size // 1024

    def at(piece, rows):
        return pl.ds(pl.multiple_of(piece * rows, 16), rows)

    order = (1, 3, 2, 0)
    steps = {}
    for k in order:
        piece = (1 - core) * 4 + lax.rem(x + k, 4)
        steps[k] = copy(packed.at[at(piece, n8)], from_core.at[k], core_sem, k, at_core())
        steps[k].start()
    waits += [steps[k] for k in order]
    x_steps = {}
    for k in order:
        steps[k].wait_recv()
        mine = packed[at(core * 4 + lax.rem(x + k, 4), n8), :].astype(F32) + from_core[k].astype(F32)
        if k:
            for_x[k] = mine.astype(BF16)
            x_steps[k] = copy(for_x.at[k], from_x.at[k - 1], x_sem, k - 1, at_x(k))
            x_steps[k].start()
    waits += [x_steps[k] for k in range(1, 4)]
    tot = mine
    for k in range(1, 4):
        x_steps[k].wait_recv()
        tot += from_x[k - 1].astype(F32)
    for_y[...] = tot.astype(BF16)

    steps = {}
    for k in (4, 3, 5, 2, 6, 1, 7):
        steps[k] = copy(for_y.at[at(lax.rem(y + k, 8), n64)], from_y.at[k - 1], y_sem, k - 1, at_y(k))
        steps[k].start()
    tot = for_y[at(y, n64), :].astype(F32)
    for k in (1, 7, 2, 6, 3, 5, 4):
        steps[k].wait_recv()
        tot += from_y[k - 1].astype(F32)
        waits.append(steps[k])
    for j in range(16):
        for_z[j] = tot[j * n1024 : (j + 1) * n1024]

    steps = {}
    spread = [8, 7, 9, 6, 10, 5, 11, 4, 12, 3, 13, 2, 14, 1, 15]
    for k in spread:
        there = lax.rem(z + k, 16)
        steps[k] = copy(for_z.at[there], from_z.at[k - 1], z_sem, k - 1, at_z(k))
        steps[k].start()
    tot = for_z[z]
    for k in reversed(spread):
        steps[k].wait_recv()
        tot += from_z[k - 1]
        waits.append(steps[k])
    final[z] = tot * inverse
    steps = {}
    for k in spread:
        steps[k] = copy(final.at[z], final.at[z], zg_sem, k - 1, at_z(k))
        steps[k].start()
    for k in reversed(spread):
        steps[k].wait_recv()
        waits.append(steps[k])

    whole = jnp.concatenate([final[j] for j in range(16)], axis=0).astype(BF16)
    group = core * 4 + x
    home = at(group * 8 + y, n64)
    gathered[home, :] = whole
    y_steps = {}
    for k in (4, 3, 5, 2, 6, 1, 7):
        y_steps[k] = copy(gathered.at[home], gathered.at[home], yg_sem, k - 1, at_y(k))
        y_steps[k].start()
    x_steps = {}
    for r in (0, 1, 7, 2, 6, 3, 5, 4):
        if r:
            y_steps[r].wait_recv()
            waits.append(y_steps[r])
        spot = at(group * 8 + lax.rem(y + 8 - r, 8), n64)
        for k in (2, 1, 3):
            x_steps[k, r] = copy(gathered.at[spot], gathered.at[spot], xg_sem, (k - 1) * 8 + r, at_x(k))
            x_steps[k, r].start()
    core_steps = {}
    for k in (0, 1, 3, 2):
        if k:
            for r in (0, 1, 7, 2, 6, 3, 5, 4):
                x_steps[k, r].wait_recv()
                waits.append(x_steps[k, r])
        spot = at(core * 4 + lax.rem(x + 4 - k, 4), n8)
        core_steps[k] = copy(gathered.at[spot], gathered.at[spot], cg_sem, k, at_core())
        core_steps[k].start()
    for k in (0, 1, 3, 2):
        core_steps[k].wait_recv()
        waits.append(core_steps[k])
    sum_ref[...] = gathered[...]
    for step in waits:
        step.wait_send()


def residual_kernel(left_ref, right_ref, sum_ref, residual_ref, projected_ref):
    share = residual_ref.shape[0]
    padded = left_ref.shape[0] // 2
    part = (share + 1) // 2
    count = left_ref.shape[1] // BLOCK
    pairs = [(i, j) for i in range(count) for j in range(i, count)]
    for p, (i, j) in enumerate(pairs):
        for h in range(2):
            tile = sum_ref[pl.ds((2 * p + h) * BLOCK, BLOCK), :]
            start = j * BLOCK + h * 128
            projected_ref[i * BLOCK : (i + 1) * BLOCK, start : start + 128] = tile
            if j > i:
                turned = jnp.transpose(tile.astype(F32)).astype(BF16)
                projected_ref[start : start + 128, i * BLOCK : (i + 1) * BLOCK] = turned
    for j in range(count):
        cut = slice(j * BLOCK, (j + 1) * BLOCK)
        out = right_ref[:, cut].astype(F32) - dot(left_ref[...], projected_ref[:, cut])
        residual_ref[:part, cut] = out[:part]
        residual_ref[part:, cut] = out[padded : padded + share - part]


def body(orbitals, potential, cell_hamiltonian, connectivity, face_nodes):
    owned, width = orbitals.shape
    cells, npc, _ = cell_hamiltonian.shape
    peers, domains = lax.axis_size("orb"), lax.axis_size("dom")
    share = owned // peers
    part = (share + 1) // 2
    padded = -(-part // 16) * 16
    end = cells * STRIDE
    orbs = peers * width
    count = orbs // BLOCK
    size = count * (count + 1) // 2 * 2 * BLOCK
    vmem = pl.BlockSpec(memory_space=pltpu.VMEM)
    steps = DEGREE + 1
    sem = pltpu.SemaphoreType.DMA
    left, right, sums = pl.pallas_call(
        functools.partial(step_kernel, (cells, npc, owned, share, 1.0 / (owned * domains))),
        out_shape=(
            jax.ShapeDtypeStruct((2 * padded, orbs), BF16),
            jax.ShapeDtypeStruct((2 * padded, orbs), BF16),
            jax.ShapeDtypeStruct((size, 128), BF16),
        ),
        in_specs=[vmem] * 5,
        out_specs=(vmem,) * 3,
        scratch_shapes=[
            pltpu.VMEM((width + 16, owned), BF16),
            pltpu.VMEM((steps, end + SIDE, width), BF16),
            pltpu.VMEM((cells, SPAN, SPAN), BF16),
            pltpu.VMEM((end + SIDE, width), F32),
            pltpu.VMEM((end, width), F32),
            pltpu.VMEM((cells, SPAN, 1), jnp.int32),
            pltpu.VMEM((cells, 1, SPAN), jnp.int32),
            pltpu.VMEM((end, 2 * width), BF16),
            pltpu.VMEM((steps, SIDE, width), BF16),
            pltpu.VMEM((steps, STRIDE, width), BF16),
            pltpu.VMEM((SIDE, SPAN), BF16),
            pltpu.VMEM((peers, part, 2 * width), BF16),
            pltpu.VMEM((peers, part, 2 * width), BF16),
            pltpu.VMEM((peers, part, 2 * width), BF16),
            pltpu.VMEM((peers, part, 2 * width), BF16),
            pltpu.VMEM((size, 128), BF16),
            pltpu.VMEM((4, size // 8, 128), BF16),
            pltpu.VMEM((4, size // 8, 128), BF16),
            pltpu.VMEM((3, size // 8, 128), BF16),
            pltpu.VMEM((size // 8, 128), BF16),
            pltpu.VMEM((7, size // 64, 128), BF16),
            pltpu.VMEM((16, size // 1024, 128), F32),
            pltpu.VMEM((15, size // 1024, 128), F32),
            pltpu.VMEM((16, size // 1024, 128), F32),
            pltpu.VMEM((size, 128), BF16),
            sem((2, 2 * steps)),
            sem((2, 1)),
            sem((2, 16)),
            sem((2, 16)),
            sem((2, 4)),
            sem((2, 3)),
            sem((2, 7)),
            sem((2, 15)),
            sem((2, 15)),
            sem((2, 7)),
            sem((2, 24)),
            sem((2, 4)),
        ],
        compiler_params=pltpu.CompilerParams(
            collective_id=0, has_side_effects=True, vmem_limit_bytes=60 << 20
        ),
        name="filter_and_project",
    )(orbitals.T, potential[None, :], cell_hamiltonian, connectivity, face_nodes[None, :])
    return pl.pallas_call(
        residual_kernel,
        out_shape=(
            jax.ShapeDtypeStruct((share, orbs), F32),
            jax.ShapeDtypeStruct((orbs, orbs), BF16),
        ),
        in_specs=[vmem] * 3,
        out_specs=(vmem, vmem),
        compiler_params=pltpu.CompilerParams(vmem_limit_bytes=60 << 20),
        name="residual",
    )(left, right, sums)


def solution(mesh):
    return jax.shard_map(
        body,
        mesh=mesh,
        in_specs=(P("dom", "orb"), P("dom"), P("dom", None, None), P("dom", None), P("dom")),
        out_specs=(P(("dom", "orb"), None), P()),
        check_vma=False,
    )
```

```python
import functools

import jax
import jax.numpy as jnp
from jax import lax
from jax.experimental import pallas as pl
from jax.experimental.pallas import tpu as pltpu
from jax.sharding import PartitionSpec as P

DEGREE = 4
MESH = pl.DeviceIdType.MESH
F32 = jnp.float32
BF16 = jnp.bfloat16

filter_center = 1.5
filter_half = 2.0

SIDE = 64
STRIDE = 320
SPAN = STRIDE + SIDE


def prefix_tables(n):
    before = lax.broadcasted_iota(jnp.int32, (n, n), 0) < lax.broadcasted_iota(jnp.int32, (n, n), 1)
    after = lax.broadcasted_iota(jnp.int32, (n, n), 0) > lax.broadcasted_iota(jnp.int32, (n, n), 1)
    return before.astype(F32).astype(BF16), after.astype(F32).astype(BF16)


def dot(a, b):
    return jnp.dot(a, b, preferred_element_type=F32)


def equal(a, b):
    return (a == b).astype(F32)


BLOCK = 256


def step_kernel(
    sizes,
    nodes_ref,
    pot_ref,
    mats_ref,
    conn_ref,
    face_ref,
    left_ref,
    right_ref,
    sum_ref,
    table,
    values,
    cellmats,
    total,
    pots,
    ids_col,
    ids_row,
    both,
    ghosts,
    behind,
    behind_mat,
    filtered_out,
    filtered_in,
    image_out,
    image_in,
    packed,
    from_core,
    for_x,
    from_x,
    for_y,
    from_y,
    for_z,
    from_z,
    final,
    gathered,
    halo_sem,
    mat_sem,
    filtered_sem,
    image_sem,
    core_sem,
    x_sem,
    y_sem,
    z_sem,
    zg_sem,
    yg_sem,
    xg_sem,
    cg_sem,
):
    cells, npc, owned, share, inverse = sizes
    dom, orb = lax.axis_index("dom"), lax.axis_index("orb")
    domains = lax.axis_size("dom")
    y, z_lo = dom // 8, lax.rem(dom, 8)
    x, z_hi, core = orb // 4, lax.rem(orb // 2, 2), lax.rem(orb, 2)
    z = z_hi * 8 + z_lo
    nxt = {"dom": lax.rem(dom + 1, domains), "orb": orb}
    prv = {"dom": lax.rem(dom + domains - 1, domains), "orb": orb}

    def at_core():
        return {"dom": dom, "orb": orb + 1 - 2 * core}

    def at_x(k):
        return {"dom": dom, "orb": lax.rem(x + k, 4) * 4 + z_hi * 2 + core}

    def at_y(k):
        return {"dom": lax.rem(y + k, 8) * 8 + z_lo, "orb": orb}

    def at_z(k):
        there = lax.rem(z + k, 16)
        return {"dom": y * 8 + lax.rem(there, 8), "orb": x * 4 + (there // 8) * 2 + core}

    def orb_at(v):
        u = lax.rem(v, 8)
        return (
            lax.rem(x + u // 2, 4) * 4 + lax.rem(z_hi + 1 - v // 8, 2) * 2 + lax.rem(core + lax.rem(u, 2), 2)
        )

    others = [v for v in range(16) if v != 8]

    def copy(src, dst, sems, k, peer):
        return pltpu.make_async_remote_copy(
            src_ref=src,
            dst_ref=dst,
            send_sem=sems.at[0, k],
            recv_sem=sems.at[1, k],
            device_id=peer,
            device_id_type=MESH,
        )

    barrier = pltpu.get_barrier_semaphore()
    peers = [prv, nxt, at_core()]
    peers += [at_x(k) for k in range(1, 4)]
    peers += [at_y(k) for k in range(1, 8)]
    peers += [at_z(k) for k in range(1, 16)]
    peers += [{"dom": dom, "orb": orb_at(v)} for v in others]
    for peer in peers:
        pl.semaphore_signal(barrier, inc=1, device_id=peer, device_id_type=MESH)

    width = values.shape[2]
    pot = pot_ref[...][None, :]
    upper = pot.astype(BF16)
    rest = pot - upper.astype(F32)
    middle = rest.astype(BF16)
    lower = (rest - middle.astype(F32)).astype(BF16)
    table[pl.ds(0, width), :] = nodes_ref[...]
    place = lax.broadcasted_iota(jnp.int32, (16, owned), 0)
    terms = jnp.where(
        place == 0,
        upper.astype(F32),
        jnp.where(place == 1, middle.astype(F32), jnp.where(place == 2, lower.astype(F32), 0.0)),
    )
    table[pl.ds(width, 16), :] = terms.astype(BF16)

    conn = conn_ref[...].astype(F32)
    turned = jnp.transpose(conn)
    rows = [conn[c : c + 1, :] for c in range(cells)]
    cols = [turned[:, c : c + 1] for c in range(cells)]
    face_row = face_ref[...].astype(F32)
    face_col = jnp.transpose(jnp.broadcast_to(face_row, (8, face_row.shape[1])))[:, :1]
    faces = face_row.shape[1]

    low = [equal(cols[c], rows[c + 1]) for c in range(cells - 1)]
    high = [equal(cols[c + 1], rows[c]) for c in range(cells - 1)]
    first_row = equal(face_col, rows[0])
    first_col = equal(cols[0], face_row)
    bottom_row = [jnp.sum(first_row, axis=0, keepdims=True)]
    bottom_row += [jnp.sum(low[c], axis=0, keepdims=True) for c in range(cells - 1)]
    bottom_col = [jnp.sum(first_col, axis=1, keepdims=True)]
    bottom_col += [jnp.sum(high[c], axis=1, keepdims=True) for c in range(cells - 1)]
    top_row = [jnp.sum(high[c], axis=0, keepdims=True) for c in range(cells - 1)]
    top_row += [(rows[-1] >= owned).astype(F32)]
    top_col = [jnp.sum(low[c], axis=1, keepdims=True) for c in range(cells - 1)]
    top_col += [(cols[-1] >= owned).astype(F32)]

    before, after = prefix_tables(npc)
    inner_row = [1.0 - bottom_row[c] - top_row[c] for c in range(cells)]
    inner_col = [1.0 - bottom_col[c] - top_col[c] for c in range(cells)]
    stacked_row = jnp.concatenate(bottom_row + inner_row, axis=0).astype(BF16)
    stacked_col = jnp.concatenate(bottom_col + inner_col, axis=1).astype(BF16)
    rank_row = dot(stacked_row, before)
    rank_col = dot(after, stacked_col)
    place_row = lax.broadcasted_iota(jnp.int32, (faces, 1), 0).astype(F32)
    place_col = lax.broadcasted_iota(jnp.int32, (1, faces), 1).astype(F32)
    low_row = [jnp.sum(first_row * place_row, axis=0, keepdims=True)]
    low_row += [rank_row[c : c + 1] for c in range(1, cells)]
    low_col = [jnp.sum(first_col * place_col, axis=1, keepdims=True)]
    low_col += [rank_col[:, c : c + 1] for c in range(1, cells)]
    high_row = [jnp.sum(high[c] * low_col[c + 1], axis=0, keepdims=True) for c in range(cells - 1)]
    high_row += [rows[-1] - owned]
    high_col = [jnp.sum(low[c] * low_row[c + 1], axis=1, keepdims=True) for c in range(cells - 1)]
    high_col += [cols[-1] - owned]

    def slots(bottom, top, low_rank, high_rank, inner_rank):
        inner = SIDE + inner_rank
        return jnp.where(bottom > 0.5, low_rank, jnp.where(top > 0.5, STRIDE + high_rank, inner)).astype(
            jnp.int32
        )

    def spread_of(c):
        slot_row = slots(
            bottom_row[c], top_row[c], low_row[c], high_row[c], rank_row[cells + c : cells + c + 1]
        )
        slot_col = slots(
            bottom_col[c], top_col[c], low_col[c], high_col[c], rank_col[:, cells + c : cells + c + 1]
        )
        down = equal(lax.broadcasted_iota(jnp.int32, (SPAN, npc), 0), slot_row)
        across = equal(slot_col, lax.broadcasted_iota(jnp.int32, (npc, SPAN), 1))
        return down, across

    def place_cell(c):
        down, across = spread_of(c)
        named = rows[c] + 1.0
        ids_col[c] = (jnp.sum(down * named, axis=1, keepdims=True) - 1.0).astype(jnp.int32)
        named = cols[c] + 1.0
        ids_row[c] = (jnp.sum(across * named, axis=0, keepdims=True) - 1.0).astype(jnp.int32)
        half = dot(down.astype(BF16), mats_ref[c]).astype(BF16)
        cellmats[c] = dot(half, across.astype(BF16)).astype(BF16)

    def take(c, carry):
        pick = equal(
            ids_col[c, pl.ds(0, STRIDE), :], lax.broadcasted_iota(jnp.int32, (STRIDE, owned), 1)
        )
        found = lax.dot_general(
            pick.astype(BF16), table[...], (((1,), (1,)), ((), ())), preferred_element_type=F32
        )
        start = pl.multiple_of(c * STRIDE, STRIDE)
        values[0, pl.ds(start, STRIDE), :] = found[:, :width].astype(BF16)
        pot = found[:, width : width + 1] + found[:, width + 1 : width + 2] + found[:, width + 2 : width + 3]
        pots[pl.ds(start, STRIDE), :] = jnp.broadcast_to(pot, (STRIDE, width))
        return carry

    end = cells * STRIDE
    waits = []

    def send(step):
        back = copy(values.at[step, pl.ds(0, SIDE)], ghosts.at[step], halo_sem, 2 * step, prv)
        ahead = copy(
            values.at[step, pl.ds(end - STRIDE, STRIDE)], behind.at[step], halo_sem, 2 * step + 1, nxt
        )
        back.start()
        ahead.start()
        waits.extend([back, ahead])
        return back, ahead

    for c in (cells - 1, 0):
        place_cell(c)
        lax.fori_loop(c, c + 1, take, 0)
    pl.semaphore_wait(barrier, len(peers))
    back, ahead = send(0)
    mat_copy = copy(cellmats.at[cells - 1, pl.ds(STRIDE, SIDE)], behind_mat, mat_sem, 0, nxt)
    mat_copy.start()
    waits.append(mat_copy)
    for c in range(1, cells - 1):
        place_cell(c)
    lax.fori_loop(1, cells - 1, take, 0)

    part = filtered_out.shape[1]
    padded = left_ref.shape[0] // 2

    def block_of(b):
        row = lax.broadcasted_iota(jnp.int32, (2 * padded, STRIDE), 0)
        low = jnp.where(row < part, row, -2 - owned)
        high = jnp.where(row < padded + share - part, row - padded + part, -2 - owned)
        target = jnp.where(row < padded, low, high) + b * share
        found = jnp.zeros((2 * padded, 2 * width), F32)
        for c in range(cells):
            pick = equal(ids_row[c, :, pl.ds(0, STRIDE)], target)
            found += dot(pick.astype(BF16), both[pl.ds(c * STRIDE, STRIDE), :])
        lane = lax.broadcasted_iota(jnp.int32, (padded, 2 * width), 1)
        return jnp.where(lane < width, found[:padded], found[padded:])[:part].astype(BF16)

    def exchange(out, into, sems):
        def one_of(v):
            there = orb_at(v)
            return copy(out.at[there], into.at[orb], sems, v, {"dom": dom, "orb": there})

        def one(v, carry):
            there = orb_at(v)
            out[there] = block_of(there)

            @pl.when(v != 0)
            def _():
                one_of(v - 1 - (v == 9).astype(jnp.int32)).start()

            return carry

        lax.fori_loop(0, 8, one, 0)
        lax.fori_loop(9, 16, one, 0)
        into[orb] = block_of(orb)
        one_of(15).start()
        return [one_of(v) for v in others]

    has_next = (dom < domains - 1).astype(F32)
    has_prev = (dom > 0).astype(F32)
    edges = [pl.ds(0, SIDE), pl.ds(end - STRIDE, STRIDE)]
    middle_rows = pl.ds(SIDE, end - STRIDE - SIDE)

    def update(step, some):
        current = values[step, some, :].astype(F32)
        image = total[some, :] + pots[some, :] * current
        if step == 0:
            values[1, some, :] = ((image - filter_center * current) / filter_half).astype(BF16)
        elif step < DEGREE:
            previous = values[step - 1, some, :].astype(F32)
            scaled = 2.0 * (image - filter_center * current) / filter_half
            values[step + 1, some, :] = (scaled - previous).astype(BF16)
        else:
            both[some, :width] = image.astype(BF16)
            both[some, width:] = image.astype(BF16)

    for step in range(DEGREE + 1):
        if step == DEGREE:
            own = pl.ds(0, end)
            both[:, :width] = values[step, own, :]
            both[:, width:] = values[step, own, :]
            filtered_steps = exchange(filtered_out, filtered_in, filtered_sem)
        total[...] = jnp.zeros_like(total)
        for c in range(cells - 1):
            span = pl.ds(c * STRIDE, SPAN)
            total[span, :] += dot(cellmats[c], values[step, span, :])
        update(step, middle_rows)
        back.wait_recv()
        values[step, pl.ds(end, SIDE), :] = (ghosts[step].astype(F32) * has_next).astype(BF16)
        span = pl.ds(end - STRIDE, SPAN)
        total[span, :] += dot(cellmats[cells - 1], values[step, span, :])
        if step == 0:
            mat_copy.wait_recv()
        ahead.wait_recv()
        shared = dot(behind_mat[:, :STRIDE], behind[step]) + dot(
            behind_mat[:, STRIDE:], values[step, pl.ds(0, SIDE), :]
        )
        total[pl.ds(0, SIDE), :] += shared * has_prev
        for some in edges:
            update(step, some)
        if step < DEGREE:
            back, ahead = send(step + 1)
    image_steps = exchange(image_out, image_in, image_sem)
    waits += filtered_steps + image_steps

    lanes = 2 * width
    lane = lax.broadcasted_iota(jnp.int32, (part, lanes), 1)

    def assemble(into, out):
        out[...] = jnp.zeros_like(out)
        for m in range(8):
            a, b = into[2 * m].astype(F32), into[2 * m + 1].astype(F32)
            cut = pl.ds(m * lanes, lanes)
            low = jnp.where(lane < width, a, pltpu.roll(b, width, 1))
            high = jnp.where(lane < width, pltpu.roll(a, width, 1), b)
            out[pl.ds(0, part), cut] = low.astype(BF16)
            out[pl.ds(padded, part), cut] = high.astype(BF16)

    for step in filtered_steps:
        step.wait_recv()
    assemble(filtered_in, left_ref)
    for step in image_steps:
        step.wait_recv()
    assemble(image_in, right_ref)

    count = left_ref.shape[1] // BLOCK
    pairs = [(i, j) for i in range(count) for j in range(i, count)]

    def multiply(first, last):
        for p in range(first, last):
            i, j = pairs[p]
            block = lax.dot_general(
                left_ref[:, i * BLOCK : (i + 1) * BLOCK],
                right_ref[:, j * BLOCK : (j + 1) * BLOCK],
                (((0,), (0,)), ((), ())),
                preferred_element_type=F32,
            ).astype(BF16)
            packed[pl.ds((2 * p) * BLOCK, BLOCK), :] = block[:, :128]
            packed[pl.ds((2 * p + 1) * BLOCK, BLOCK), :] = block[:, 128:]

    half_way = len(pairs) // 2

    @pl.when(core == 0)
    def _():
        multiply(half_way, len(pairs))

    @pl.when(core == 1)
    def _():
        multiply(0, half_way)

    size = packed.shape[0]
    n2, n8, n64, n1024 = size // 2, size // 8, size // 64, size // 1024

    def at(piece, rows):
        return pl.ds(pl.multiple_of(piece * rows, 16), rows)

    order = (1, 3, 2, 0)
    steps = {}
    for k in order:
        piece = (1 - core) * 4 + lax.rem(x + k, 4)
        steps[k] = copy(packed.at[at(piece, n8)], from_core.at[k], core_sem, k, at_core())
        steps[k].start()
    waits += [steps[k] for k in order]

    @pl.when(core == 0)
    def _():
        multiply(0, half_way)

    @pl.when(core == 1)
    def _():
        multiply(half_way, len(pairs))

    x_steps = {}
    for k in order:
        steps[k].wait_recv()
        mine = packed[at(core * 4 + lax.rem(x + k, 4), n8), :].astype(F32) + from_core[k].astype(F32)
        if k:
            for_x[k] = mine.astype(BF16)
            x_steps[k] = copy(for_x.at[k], from_x.at[k - 1], x_sem, k - 1, at_x(k))
            x_steps[k].start()
    waits += [x_steps[k] for k in range(1, 4)]
    tot = mine
    for k in range(1, 4):
        x_steps[k].wait_recv()
        tot += from_x[k - 1].astype(F32)
    for_y[...] = tot.astype(BF16)

    steps = {}
    for k in (4, 3, 5, 2, 6, 1, 7):
        steps[k] = copy(for_y.at[at(lax.rem(y + k, 8), n64)], from_y.at[k - 1], y_sem, k - 1, at_y(k))
        steps[k].start()
    tot = for_y[at(y, n64), :].astype(F32)
    for k in (1, 7, 2, 6, 3, 5, 4):
        steps[k].wait_recv()
        tot += from_y[k - 1].astype(F32)
        waits.append(steps[k])
    for j in range(16):
        for_z[j] = tot[j * n1024 : (j + 1) * n1024]

    steps = {}
    spread = [8, 7, 9, 6, 10, 5, 11, 4, 12, 3, 13, 2, 14, 1, 15]
    for k in spread:
        there = lax.rem(z + k, 16)
        steps[k] = copy(for_z.at[there], from_z.at[k - 1], z_sem, k - 1, at_z(k))
        steps[k].start()
    tot = for_z[z]
    for k in reversed(spread):
        steps[k].wait_recv()
        tot += from_z[k - 1]
        waits.append(steps[k])
    final[z] = tot * inverse
    steps = {}
    for k in spread:
        steps[k] = copy(final.at[z], final.at[z], zg_sem, k - 1, at_z(k))
        steps[k].start()
    for k in reversed(spread):
        steps[k].wait_recv()
        waits.append(steps[k])

    whole = jnp.concatenate([final[j] for j in range(16)], axis=0).astype(BF16)
    group = core * 4 + x
    home = at(group * 8 + y, n64)
    gathered[home, :] = whole
    y_steps = {}
    for k in (4, 3, 5, 2, 6, 1, 7):
        y_steps[k] = copy(gathered.at[home], gathered.at[home], yg_sem, k - 1, at_y(k))
        y_steps[k].start()
    x_steps = {}
    for r in (0, 1, 7, 2, 6, 3, 5, 4):
        if r:
            y_steps[r].wait_recv()
            waits.append(y_steps[r])
        spot = at(group * 8 + lax.rem(y + 8 - r, 8), n64)
        for k in (2, 1, 3):
            x_steps[k, r] = copy(gathered.at[spot], gathered.at[spot], xg_sem, (k - 1) * 8 + r, at_x(k))
            x_steps[k, r].start()
    core_steps = {}
    for k in (0, 1, 3, 2):
        if k:
            for r in (0, 1, 7, 2, 6, 3, 5, 4):
                x_steps[k, r].wait_recv()
                waits.append(x_steps[k, r])
        spot = at(core * 4 + lax.rem(x + 4 - k, 4), n8)
        core_steps[k] = copy(gathered.at[spot], gathered.at[spot], cg_sem, k, at_core())
        core_steps[k].start()
    for k in (0, 1, 3, 2):
        core_steps[k].wait_recv()
        waits.append(core_steps[k])
    sum_ref[...] = gathered[...]
    for step in waits:
        step.wait_send()


def residual_kernel(left_ref, right_ref, sum_ref, residual_ref, projected_ref):
    share = residual_ref.shape[0]
    padded = left_ref.shape[0] // 2
    part = (share + 1) // 2
    count = left_ref.shape[1] // BLOCK
    pairs = [(i, j) for i in range(count) for j in range(i, count)]
    for p, (i, j) in enumerate(pairs):
        for h in range(2):
            tile = sum_ref[pl.ds((2 * p + h) * BLOCK, BLOCK), :]
            start = j * BLOCK + h * 128
            projected_ref[i * BLOCK : (i + 1) * BLOCK, start : start + 128] = tile
            if j > i:
                turned = jnp.transpose(tile.astype(F32)).astype(BF16)
                projected_ref[start : start + 128, i * BLOCK : (i + 1) * BLOCK] = turned
    for j in range(count):
        cut = slice(j * BLOCK, (j + 1) * BLOCK)
        out = right_ref[:, cut].astype(F32) - dot(left_ref[...], projected_ref[:, cut])
        residual_ref[:part, cut] = out[:part]
        residual_ref[part:, cut] = out[padded : padded + share - part]


def body(orbitals, potential, cell_hamiltonian, connectivity, face_nodes):
    owned, width = orbitals.shape
    cells, npc, _ = cell_hamiltonian.shape
    peers, domains = lax.axis_size("orb"), lax.axis_size("dom")
    share = owned // peers
    part = (share + 1) // 2
    padded = -(-part // 16) * 16
    end = cells * STRIDE
    orbs = peers * width
    count = orbs // BLOCK
    size = count * (count + 1) // 2 * 2 * BLOCK
    vmem = pl.BlockSpec(memory_space=pltpu.VMEM)
    steps = DEGREE + 1
    sem = pltpu.SemaphoreType.DMA
    left, right, sums = pl.pallas_call(
        functools.partial(step_kernel, (cells, npc, owned, share, 1.0 / (owned * domains))),
        out_shape=(
            jax.ShapeDtypeStruct((2 * padded, orbs), BF16),
            jax.ShapeDtypeStruct((2 * padded, orbs), BF16),
            jax.ShapeDtypeStruct((size, 128), BF16),
        ),
        in_specs=[vmem] * 5,
        out_specs=(vmem,) * 3,
        scratch_shapes=[
            pltpu.VMEM((width + 16, owned), BF16),
            pltpu.VMEM((steps, end + SIDE, width), BF16),
            pltpu.VMEM((cells, SPAN, SPAN), BF16),
            pltpu.VMEM((end + SIDE, width), F32),
            pltpu.VMEM((end, width), F32),
            pltpu.VMEM((cells, SPAN, 1), jnp.int32),
            pltpu.VMEM((cells, 1, SPAN), jnp.int32),
            pltpu.VMEM((end, 2 * width), BF16),
            pltpu.VMEM((steps, SIDE, width), BF16),
            pltpu.VMEM((steps, STRIDE, width), BF16),
            pltpu.VMEM((SIDE, SPAN), BF16),
            pltpu.VMEM((peers, part, 2 * width), BF16),
            pltpu.VMEM((peers, part, 2 * width), BF16),
            pltpu.VMEM((peers, part, 2 * width), BF16),
            pltpu.VMEM((peers, part, 2 * width), BF16),
            pltpu.VMEM((size, 128), BF16),
            pltpu.VMEM((4, size // 8, 128), BF16),
            pltpu.VMEM((4, size // 8, 128), BF16),
            pltpu.VMEM((3, size // 8, 128), BF16),
            pltpu.VMEM((size // 8, 128), BF16),
            pltpu.VMEM((7, size // 64, 128), BF16),
            pltpu.VMEM((16, size // 1024, 128), F32),
            pltpu.VMEM((15, size // 1024, 128), F32),
            pltpu.VMEM((16, size // 1024, 128), F32),
            pltpu.VMEM((size, 128), BF16),
            sem((2, 2 * steps)),
            sem((2, 1)),
            sem((2, 16)),
            sem((2, 16)),
            sem((2, 4)),
            sem((2, 3)),
            sem((2, 7)),
            sem((2, 15)),
            sem((2, 15)),
            sem((2, 7)),
            sem((2, 24)),
            sem((2, 4)),
        ],
        compiler_params=pltpu.CompilerParams(
            collective_id=0, has_side_effects=True, vmem_limit_bytes=60 << 20
        ),
        name="filter_and_project",
    )(orbitals.T, potential, cell_hamiltonian, connectivity, face_nodes[None, :])
    return pl.pallas_call(
        residual_kernel,
        out_shape=(
            jax.ShapeDtypeStruct((share, orbs), F32),
            jax.ShapeDtypeStruct((orbs, orbs), BF16),
        ),
        in_specs=[vmem] * 3,
        out_specs=(vmem, vmem),
        compiler_params=pltpu.CompilerParams(vmem_limit_bytes=60 << 20),
        name="residual",
    )(left, right, sums)


def solution(mesh):
    return jax.shard_map(
        body,
        mesh=mesh,
        in_specs=(P("dom", "orb"), P("dom"), P("dom", None, None), P("dom", None), P("dom")),
        out_specs=(P(("dom", "orb"), None), P()),
        check_vma=False,
    )
```
